128 devices in a mesh: gx: 8 (over z, x_hi), gy: 4 (over y), gz: 4 (over x_lo, core).
Axes of the slice: x: 4 (x_hi: 2, x_lo: 2; x = x_hi * 2 + x_lo), y: 4, z: 4, core: 2. Of those that a mesh axis runs over, the one named last changes fastest.
Arguments:
- state: float32 [53, 32, 16, 512], P(None, 'gx', 'gy', 'gz'), may hold values from -8 to 8
- diffusivity: float32 [53], replicated, may hold values from 0.01 to 0.08
- rates: float32 [53, 53], replicated, may hold values from -1.75 to 1.75
- inverse: float32 [53, 53, 32, 16, 512], P(None, None, 'gx', 'gy', 'gz'), may hold values from -3 to 5
- boundary: int32 [3], replicated, may hold values from 0 to 1, as said below
Outputs:
- new_state: float32 [53, 32, 16, 512], P(None, 'gx', 'gy', 'gz')
The draws below stay inside these ranges and needn't reach their ends.
Inputs may be any that keep to these rules, and one draw needn't show every extreme that they name: `boundary`: 1 marks a dimension with periodic faces, 0 one with mirrored walls; at least one dimension has each kind.
All inputs are finite; a program needn't handle non-finite values.
Results may differ from the reference program's by a relative error of at most 0.00014.
Values sent between devices are 32-bit elements; how exact they have to be, the bound alone decides.
A program may use at most 128 MiB of HBM per device.

```python
import math
import jax
import jax.numpy as jnp
from jax import lax

S = 53
NEWTON = 2
NX = 32
NY = 16
NZ = 512


def draw_state(key, part):
    position = jnp.arange(NX, dtype=jnp.float32) / max(NX - 1, 1)
    growth = (1.0 + 2.0 * position)[None, :, None, None]
    rough = jax.random.truncated_normal(key, -4.0, 4.0, (S, NX, NY, NZ), jnp.float32)
    return rough * growth * 0.6


def draw_inverse(key, part):
    key_noise, key_diag = jax.random.split(jax.random.fold_in(key, 7), 2)
    noise = jax.random.truncated_normal(key_noise, -4.0, 4.0, (S, S, NX, NY, NZ), jnp.float32) * (0.4 / math.sqrt(S))
    diagonal = jax.random.uniform(key_diag, (S, 1, NX, NY, NZ), jnp.float32, 0.7, 1.3)
    identity = jnp.eye(S, dtype=jnp.float32)[:, :, None, None, None]
    matrix = identity * diagonal + noise
    return matrix


def draw_boundary(key, part):
    key_extra, key_order = jax.random.split(jax.random.fold_in(key, 11))
    extra = jax.random.randint(key_extra, (1,), 0, 2, jnp.int32)
    kinds = jnp.concatenate([jnp.array([0, 1], jnp.int32), extra])
    return jax.random.permutation(key_order, kinds).astype(jnp.int32)


def centred(own_key, dims, width, limit, kind=jnp.bfloat16):
    return jnp.clip(width * jax.random.normal(own_key, dims, jnp.float32), -limit, limit).astype(kind)


def setup_inputs(seed: int = 0) -> dict:
    arg_keys = jax.random.split(jax.random.key(seed), 6)
    return {
        "state": draw_state(jax.random.fold_in(arg_keys[5], 71), 0),
        "diffusivity": jnp.clip(jnp.exp(jax.random.uniform(arg_keys[1], (S,), jnp.float32, math.log(0.01), math.log(0.08))), 0.01, 0.08),
        "rates": centred(arg_keys[2], (S, S), (S // 4) ** -0.5, 1.75, jnp.float32),
        "inverse": draw_inverse(jax.random.fold_in(arg_keys[5], 71), 0),
        "boundary": draw_boundary(jax.random.fold_in(arg_keys[5], 71), 0),
    }


implicit_gamma = 0.2928932188134524
explicit_delta = -0.7071067811865475
rel_tol = 0.1
abs_tol = 0.05
drift_speed = 0.2

def extend_dim(field, dim, periodic):
    widths = [(0, 0)] * 4
    widths[dim] = (2, 2)
    cyclic = jnp.pad(field, widths, mode='wrap')
    mirror = jnp.pad(field, widths, mode='symmetric')
    return jnp.where(periodic, cyclic, mirror)

def stencil_terms(extended, dim):
    length = extended.shape[dim] - 4
    parts = [lax.slice_in_dim(extended, k, k + length, axis=dim) for k in range(5)]
    second = (-parts[0] + 16.0 * parts[1] - 30.0 * parts[2] + 16.0 * parts[3] - parts[4]) / 12.0
    return (second, parts[1])

def transport(field, diffusivity, boundary):
    lap_x, below_x = stencil_terms(extend_dim(field, 1, boundary[0] == 1), 1)
    lap_y, unused_y = stencil_terms(extend_dim(field, 2, boundary[1] == 1), 2)
    lap_z, unused_z = stencil_terms(extend_dim(field, 3, boundary[2] == 1), 3)
    return diffusivity[:, None, None, None] * (lap_x + lap_y + lap_z) - drift_speed * (field - below_x)

def chemistry(field, rates):
    return jnp.einsum('sj,jxyz->sxyz', rates, jnp.tanh(field), precision=lax.Precision.HIGHEST)

def newton_solve(base, inverse, rates, weights):
    guess = base
    for sweep in range(NEWTON):
        residual = guess - base - implicit_gamma * chemistry(guess, rates)
        update = jnp.einsum('sjxyz,jxyz->sxyz', inverse, residual, precision=lax.Precision.HIGHEST)
        norm_value = jnp.sqrt(jnp.mean(jnp.square(update * weights)))
        guess = guess - update / jnp.maximum(norm_value, 1.0)
    return guess

def reference(state, diffusivity, rates, inverse, boundary):
    weights = 1.0 / (rel_tol * jnp.abs(state) + abs_tol)
    first_rate = transport(state, diffusivity, boundary)
    section = newton_solve(state + implicit_gamma * first_rate, inverse, rates, weights)
    second_rate = transport(section, diffusivity, boundary)
    base = state + explicit_delta * first_rate + (1.0 - explicit_delta) * second_rate
    base = base + (1.0 - implicit_gamma) * chemistry(section, rates)
    return newton_solve(base, inverse, rates, weights)
```

```python
import functools
import itertools

import jax
import jax.numpy as jnp
from jax import lax
from jax.experimental import pallas as pl
from jax.experimental.pallas import tpu as pltpu
from jax.sharding import PartitionSpec as P

MESH = pl.DeviceIdType.MESH
AXES = ("gx", "gy", "gz")

GAMMA = 0.2928932188134524
DELTA = -0.7071067811865475
REL_TOL = 0.1
ABS_TOL = 0.05
DRIFT = 0.2

S = 53
SP = 64
R = 16
L = 128
GROUP = 8
CHUNKS = 8


def offsets(sizes):
    out = []
    for off in itertools.product(*[range(n) for n in sizes]):
        if any(off):
            out.append(off)

    def hops(off):
        gx, gy, gz = off
        ring = lambda d, n: min(d % n, n - d % n)
        far_y = ring(gy, sizes[1])
        far_z = ring(gx // 2, sizes[0] // 2)
        far_x = ring(2 * (gx % 2) + gz // 2, 4)
        return far_x + far_y + far_z

    return sorted(out, key=lambda off: -hops(off))


def species_loop(fn, block=4):
    whole = S // block

    def body(i, carry):
        for k in range(block):
            fn(i * block + k)
        return carry

    lax.fori_loop(0, whole, body, 0)
    for s in range(whole * block, S):
        fn(s)


def kernel(
    sizes,
    state_hbm, diff_ref, rates_ref, inv_hbm, bound_ref,
    out_ref,
    st, inv, xlo, xhi, ya, yb, yra, yrb, zp, zlo, zhi,
    e0, ebuf, wts, base, zed, dee, gee, tbuf, cbuf, rpad, rows,
    load_sem, inv_sem, halo_send, halo_recv, norm_send, norm_recv,
):
    n_all = sizes[0] * sizes[1] * sizes[2]
    entries = float(S * R * L * n_all)
    pos = [lax.axis_index(a) for a in AXES]
    me = (pos[0] * sizes[1] + pos[1]) * sizes[2] + pos[2]

    def at(off):
        return {a: lax.rem(p + o, n) for a, p, o, n in zip(AXES, pos, off, sizes)}

    peers = offsets(sizes)

    load = pltpu.make_async_copy(state_hbm, st, load_sem)
    load.start()
    per = -(-S // CHUNKS)
    inv_loads = []
    for c in range(CHUNKS):
        lo, hi = c * per, min(S, (c + 1) * per)
        cp = pltpu.make_async_copy(inv_hbm.at[pl.ds(lo, hi - lo)], inv.at[pl.ds(lo, hi - lo)], inv_sem.at[c])
        cp.start()
        inv_loads.append(cp)

    barrier = pltpu.get_barrier_semaphore()
    for off in peers:
        pl.semaphore_signal(barrier, inc=1, device_id=at(off), device_id_type=MESH)

    row = lax.broadcasted_iota(jnp.int32, (8, L), 0)
    lane = lax.broadcasted_iota(jnp.int32, (8, L), 1)
    yy = lax.rem(row, 4)
    pp = lax.rem(lane, 4)
    f = lambda c: jnp.where(c, 1.0, 0.0).astype(jnp.float32)
    low_rows = f(row < 4)
    high_rows = f(row >= 4)

    def wall(d, edge):
        return jnp.where((bound_ref[d] == 0) & (pos[d] == edge), 1.0, 0.0).astype(jnp.float32)

    wx0, wx1 = wall(0, 0), wall(0, sizes[0] - 1)
    wy0, wy1 = wall(1, 0), wall(1, sizes[1] - 1)
    wz0, wz1 = wall(2, 0), wall(2, sizes[2] - 1)
    mx0, mx1, my0, my1, mz0, mz1 = [1.0 - w for w in (wx0, wx1, wy0, wy1, wz0, wz1)]

    rd = lambda ref, s, h: ref[s, pl.ds(8 * h, 8), :]

    def pack(field):
        def one(s):
            v0, v1 = rd(field, s, 0), rd(field, s, 1)
            ya[s] = jnp.where(yy < 2, pltpu.roll(v0, 6, 0), v1)
            yb[s] = jnp.where(yy < 2, v0, pltpu.roll(v1, 2, 0))

        species_loop(one)
        grp = lane // 4
        for q in range(4):
            h, s0 = q % 2, 32 * (q // 2)

            def body(k, acc):
                v = rd(field, s0 + k, h)
                return jnp.where(grp == k, pltpu.roll(v, 4 * k + 2, 1), acc)

            zp[pl.ds(8 * q, 8), :] = lax.fori_loop(0, min(32, S - s0), body, jnp.zeros((8, L), jnp.float32))

    def halo_copies(field, k):
        nx, ny, nz = sizes
        todo = [
            (field.at[:, pl.ds(8, 8), :], xlo.at[k], (1, 0, 0)),
            (field.at[:, pl.ds(0, 8), :], xhi.at[k], (nx - 1, 0, 0)),
            (ya, yra.at[k], (0, 1, 0)),
            (yb, yrb.at[k], (0, ny - 1, 0)),
            (zp, zlo.at[k], (0, 0, 1)),
            (zp, zhi.at[k], (0, 0, nz - 1)),
        ]
        cps = []
        for i, (src, dst, off) in enumerate(todo):
            cps.append(pltpu.make_async_remote_copy(
                src_ref=src, dst_ref=dst, send_sem=halo_send.at[k, i], recv_sem=halo_recv.at[k, i],
                device_id=at(off), device_id_type=MESH))
        return cps

    def inner(field, out):
        x0c = -30.0 + 16.0 * wx0 * low_rows
        x1c = -30.0 + 16.0 * wx1 * high_rows
        b1 = 16.0 * f(yy >= 1) - wy0 * f(yy == 1) - wy1 * f(yy == 3)
        bm1 = 16.0 * f(yy <= 2) - wy0 * f(yy == 0) - wy1 * f(yy == 2)
        b2, bm2 = -f(yy >= 2), -f(yy <= 1)
        a1 = 16.0 * f(lane >= 1) - wz0 * f(lane == 1) - wz1 * f(lane == L - 1)
        am1 = 16.0 * f(lane <= L - 2) - wz0 * f(lane == 0) - wz1 * f(lane == L - 2)
        a2, am2 = -f(lane >= 2), -f(lane <= L - 3)
        yz0 = (-60.0 + 16.0 * wy0 * f(yy == 0) + 16.0 * wy1 * f(yy == 3)
               + 16.0 * wz0 * f(lane == 0) + 16.0 * wz1 * f(lane == L - 1))
        own_drift = -DRIFT + DRIFT * wx0 * low_rows

        def one(s):
            c = diff_ref[s] * (1.0 / 12.0)
            v0, v1 = rd(field, s, 0), rd(field, s, 1)
            s0, s1 = pltpu.roll(v0, 4, 0), pltpu.roll(v1, 4, 0)

            def yz(v):
                return (yz0 * v + b1 * pltpu.roll(v, 1, 0) + b2 * pltpu.roll(v, 2, 0)
                        + bm1 * pltpu.roll(v, 7, 0) + bm2 * pltpu.roll(v, 6, 0)
                        + a1 * pltpu.roll(v, 1, 1) + a2 * pltpu.roll(v, 2, 1)
                        + am1 * pltpu.roll(v, L - 1, 1) + am2 * pltpu.roll(v, L - 2, 1))

            l0 = x0c * v0 + (16.0 - wx0) * s0 + 16.0 * high_rows * s1 - v1 + yz(v0)
            l1 = x1c * v1 + (16.0 - wx1) * s1 + 16.0 * low_rows * s0 - v0 + yz(v1)
            out[s, pl.ds(0, 8), :] = c * l0 + own_drift * v0 + DRIFT * high_rows * s0
            out[s, pl.ds(8, 8), :] = c * l1 - DRIFT * v1 + DRIFT * jnp.where(row >= 4, s1, s0)

        species_loop(one, 2)

    def outer(k, part, fin):
        edge = (lane < 2) | (lane >= L - 2)
        for q in range(4):
            lo = zlo[k, pl.ds(8 * q, 8), :]
            hi = zhi[k, pl.ds(8 * q, 8), :]
            from_hi = mz1 * (16.0 * f(pp == 1) * pltpu.roll(hi, L - 1, 1) - pltpu.roll(hi, L - 2, 1))
            from_lo = mz0 * (16.0 * f(pp == 2) * pltpu.roll(lo, 1, 1) - pltpu.roll(lo, 2, 1))
            zp[pl.ds(8 * q, 8), :] = jnp.where(pp < 2, from_hi, from_lo)
        even = 16.0 * my0 * f(lax.rem(row, 2) == 0)
        odd = 16.0 * my1 * f(lax.rem(row, 2) == 1)
        lo16, hi16, dr = 16.0 * mx0 * low_rows, 16.0 * mx1 * high_rows, DRIFT * mx0 * low_rows

        def one(s):
            c = diff_ref[s] * (1.0 / 12.0)
            xl, xh = xlo[k, s], xhi[k, s]
            a, b = yra[k, s], yrb[k, s]
            rl, rh = pltpu.roll(xl, 4, 0), pltpu.roll(xh, 4, 0)
            ca = even * pltpu.roll(a, 7, 0) - my0 * a
            cb = odd * pltpu.roll(b, 1, 0) - my1 * b
            q = 2 * (s // 32)
            g = lax.rem(s, 32)
            shift = lax.rem(2 * L - 2 - 4 * g, L)
            off = q * 8 if isinstance(q, int) else pl.multiple_of(q * 8, 8)
            z0 = pltpu.roll(zp[pl.ds(off, 8), :], shift, 1)
            z1 = pltpu.roll(zp[pl.ds(off + 8, 8), :], shift, 1)
            l0 = lo16 * rl - mx0 * xl + jnp.where(yy < 2, ca, pltpu.roll(cb, 2, 0)) + jnp.where(edge, z0, 0.0)
            l1 = hi16 * rh - mx1 * xh + jnp.where(yy < 2, pltpu.roll(ca, 6, 0), cb) + jnp.where(edge, z1, 0.0)
            fin(s, 0, rd(part, s, 0) + c * l0 + dr * rl)
            fin(s, 1, rd(part, s, 1) + c * l1)

        species_loop(one, 2)

    def put_tanh(s, h, v):
        start = s * R + 8 * h
        if not isinstance(s, int):
            start = pl.multiple_of(start, 8)
        tbuf[pl.ds(start, 8), :] = jnp.tanh(v)

    def chem_at(s, h):
        start = s * R + 8 * h
        if not isinstance(s, int):
            start = pl.multiple_of(start, 8)
        return cbuf[pl.ds(start, 8), :]

    def chemistry():
        lhs = rows_lhs()
        for r in range(0, R, 2):
            t = jnp.concatenate([tbuf[pl.ds(r + i, SP, stride=R), :] for i in range(2)], axis=1)
            hi = t.astype(jnp.bfloat16)
            lo = (t - hi.astype(jnp.float32)).astype(jnp.bfloat16)
            got = jnp.dot(lhs, jnp.concatenate([hi, lo, hi, lo], axis=0), preferred_element_type=jnp.float32)
            for i in range(2):
                cbuf[pl.ds(r + i, SP, stride=R), :] = got[:, i * L:(i + 1) * L]

    def rows_lhs():
        both = rpad[...] + pltpu.roll(rpad[...], SP, 1)
        hi = both.astype(jnp.bfloat16)
        lo = (both - hi.astype(jnp.float32)).astype(jnp.bfloat16)
        return jnp.concatenate([hi, lo], axis=1)

    def matvec():
        last = S - GROUP
        steps = -(-S // GROUP)

        def body(i, carry):
            h = lax.rem(i, 2)
            s0 = jnp.minimum((i // 2) * GROUP, last)
            at_rows = pl.ds(pl.multiple_of(h * 8, 8), 8)
            acc = None
            for j in range(S):
                term = inv[pl.ds(s0, GROUP), j, at_rows, :] * gee[j, at_rows, :][None]
                acc = term if acc is None else acc + term
            dee[pl.ds(s0, GROUP), at_rows, :] = acc
            return carry

        lax.fori_loop(0, 2 * steps, body, 0)

    def damping(k):
        def body(s, acc):
            u = dee[s] * wts[s]
            u = u * u
            return acc + u[0:8] + u[8:16]

        acc = lax.fori_loop(0, S, body, jnp.zeros((8, L), jnp.float32))
        rows[k, pl.ds(me, 1), :] = jnp.sum(acc, axis=0, keepdims=True)
        for off in peers:
            pltpu.make_async_remote_copy(
                src_ref=rows.at[k, pl.ds(me, 1), :], dst_ref=rows.at[k, pl.ds(me, 1), :],
                send_sem=norm_send.at[k], recv_sem=norm_recv.at[k],
                device_id=at(off), device_id_type=MESH).start()
        count = len(peers)
        all_rows = pltpu.make_async_remote_copy(
            src_ref=rows.at[k, pl.ds(0, count), :], dst_ref=rows.at[k, pl.ds(0, count), :],
            send_sem=norm_send.at[k], recv_sem=norm_recv.at[k],
            device_id=at(peers[0]), device_id_type=MESH)
        all_rows.wait_recv()
        all_rows.wait_send()
        total = jnp.sum(jnp.sum(rows[k], axis=0, keepdims=True), axis=1, keepdims=True)
        return 1.0 / jnp.maximum(jnp.sqrt(total * (1.0 / entries)), 1.0)

    halves = [(0, pl.ds(0, 8)), (1, pl.ds(8, 8))]

    def newton(k, last):
        chemistry()

        def first(s):
            for h, hs in halves:
                gee[s, hs, :] = -GAMMA * chem_at(s, h)

        species_loop(first)
        if k == 0:
            for cp in inv_loads:
                cp.wait()
        matvec()
        r = damping(k)

        def mid(s):
            for h, hs in halves:
                z = base[s, hs, :] - dee[s, hs, :] * r
                zed[s, hs, :] = z
                put_tanh(s, h, z)

        species_loop(mid)
        chemistry()

        def second(s):
            for h, hs in halves:
                gee[s, hs, :] = zed[s, hs, :] - base[s, hs, :] - GAMMA * chem_at(s, h)

        species_loop(second)
        matvec()
        r2 = damping(k + 1)

        def end(s):
            for h, hs in halves:
                last(s, h, zed[s, hs, :] - dee[s, hs, :] * r2)

        species_loop(end)

    tbuf[pl.ds(S * R, (SP - S) * R), :] = jnp.zeros(((SP - S) * R, L), jnp.float32)
    rpad[...] = jnp.zeros((SP, L), jnp.float32)
    rpad[0:S, 0:S] = rates_ref[...]
    load.wait()
    pack(st)
    pl.semaphore_wait(barrier, len(peers))
    cps = halo_copies(st, 0)
    for cp in cps:
        cp.start()
    inner(st, e0)

    def weigh(s):
        wts[s] = 1.0 / (REL_TOL * jnp.abs(st[s]) + ABS_TOL)

    species_loop(weigh)
    for cp in cps:
        cp.wait()

    def fin0(s, h, e):
        hs = pl.ds(8 * h, 8)
        e0[s, hs, :] = e
        b = st[s, hs, :] + GAMMA * e
        base[s, hs, :] = b
        put_tanh(s, h, b)

    outer(0, e0, fin0)

    def keep(s, h, v):
        gee[s, pl.ds(8 * h, 8), :] = v
        put_tanh(s, h, v)

    newton(0, keep)

    pack(gee)
    cps = halo_copies(gee, 1)
    for cp in cps:
        cp.start()
    inner(gee, ebuf)
    chemistry()

    def pre(s):
        for h, hs in halves:
            base[s, hs, :] = st[s, hs, :] + DELTA * e0[s, hs, :] + (1.0 - GAMMA) * chem_at(s, h)

    species_loop(pre)
    for cp in cps:
        cp.wait()

    def fin1(s, h, e):
        hs = pl.ds(8 * h, 8)
        b = base[s, hs, :] + (1.0 - DELTA) * e
        base[s, hs, :] = b
        put_tanh(s, h, b)

    outer(1, ebuf, fin1)

    def give(s, h, v):
        out_ref[s, pl.ds(8 * h, 8), :] = v

    newton(2, give)


def body(sizes, state, diffusivity, rates, inverse, boundary):
    shape = state.shape
    field = pltpu.VMEM((S, R, L), jnp.float32)
    face = pltpu.VMEM((S, 8, L), jnp.float32)
    faces = pltpu.VMEM((2, S, 8, L), jnp.float32)
    n_all = sizes[0] * sizes[1] * sizes[2]
    out = pl.pallas_call(
        functools.partial(kernel, sizes),
        name="ark_step",
        out_shape=jax.ShapeDtypeStruct((S, R, L), jnp.float32),
        in_specs=[
            pl.BlockSpec(memory_space=pl.ANY),
            pl.BlockSpec(memory_space=pltpu.SMEM),
            pl.BlockSpec(memory_space=pltpu.VMEM),
            pl.BlockSpec(memory_space=pl.ANY),
            pl.BlockSpec(memory_space=pltpu.SMEM),
        ],
        out_specs=pl.BlockSpec(memory_space=pltpu.VMEM),
        scratch_shapes=[
            field, pltpu.VMEM((S, S, R, L), jnp.float32),
            faces, faces, face, face, faces, faces,
            pltpu.VMEM((32, L), jnp.float32), pltpu.VMEM((2, 32, L), jnp.float32), pltpu.VMEM((2, 32, L), jnp.float32),
            field, field, field, field, field, field, field,
            pltpu.VMEM((SP * R, L), jnp.float32), pltpu.VMEM((SP * R, L), jnp.float32),
            pltpu.VMEM((SP, L), jnp.float32), pltpu.VMEM((4, n_all, L), jnp.float32),
            pltpu.SemaphoreType.DMA, pltpu.SemaphoreType.DMA((CHUNKS,)),
            pltpu.SemaphoreType.DMA((2, 6)), pltpu.SemaphoreType.DMA((2, 6)),
            pltpu.SemaphoreType.DMA((4,)), pltpu.SemaphoreType.DMA((4,)),
        ],
        compiler_params=pltpu.CompilerParams(collective_id=0, has_side_effects=True),
    )(
        state.reshape(S, R, L), diffusivity, rates, inverse.reshape(S, S, R, L), boundary,
    )
    return out.reshape(shape)


def solution(mesh):
    sizes = tuple(mesh.shape[a] for a in AXES)
    in_specs = (P(None, "gx", "gy", "gz"), P(), P(), P(None, None, "gx", "gy", "gz"), P())
    return jax.shard_map(
        functools.partial(body, sizes), mesh=mesh, in_specs=in_specs, out_specs=P(None, "gx", "gy", "gz"), check_vma=False)
```

```python
import functools
import itertools

import jax
import jax.numpy as jnp
from jax import lax
from jax.experimental import pallas as pl
from jax.experimental.pallas import tpu as pltpu
from jax.sharding import PartitionSpec as P

MESH = pl.DeviceIdType.MESH
AXES = ("gx", "gy", "gz")

GAMMA = 0.2928932188134524
DELTA = -0.7071067811865475
REL_TOL = 0.1
ABS_TOL = 0.05
DRIFT = 0.2

S = 53
SP = 64
R = 16
L = 128
GROUP = 9
JB = 8
CHUNKS = 8


def offsets(sizes):
    out = []
    for off in itertools.product(*[range(n) for n in sizes]):
        if any(off):
            out.append(off)

    def hops(off):
        gx, gy, gz = off
        ring = lambda d, n: min(d % n, n - d % n)
        far_y = ring(gy, sizes[1])
        far_z = ring(gx // 2, sizes[0] // 2)
        far_x = ring(2 * (gx % 2) + gz // 2, 4)
        return far_x + far_y + far_z

    return sorted(out, key=lambda off: -hops(off))


def species_loop(fn, block=4):
    whole = S // block

    def body(i, carry):
        for k in range(block):
            fn(i * block + k)
        return carry

    lax.fori_loop(0, whole, body, 0)
    for s in range(whole * block, S):
        fn(s)


def block_loop(fn, block=16):
    whole = S // block

    def body(i, carry):
        fn(i, [i * block + k for k in range(block)])
        return carry

    lax.fori_loop(0, whole, body, 0)
    fn(whole, list(range(whole * block, S)))


def tile8(i):
    return pl.ds(8 * i if isinstance(i, int) else pl.multiple_of(8 * i, 8), 8)


def kernel(
    sizes,
    state_hbm, diff_ref, rates_ref, inv_hbm, bound_ref,
    out_ref,
    st, inv, xlo, xhi, ya, yb, yra, yrb, zp, zk, zlo, zhi,
    e0, ebuf, wts, base, zed, sec, dee, gee, tbuf, cbuf, rpad, rows,
    load_sem, inv_sem, halo_send, halo_recv, norm_send, norm_recv, ready,
):
    n_all = sizes[0] * sizes[1] * sizes[2]
    entries = float(S * R * L * n_all)
    pos = [lax.axis_index(a) for a in AXES]
    me = (pos[0] * sizes[1] + pos[1]) * sizes[2] + pos[2]

    def at(off):
        return {a: lax.rem(p + o, n) for a, p, o, n in zip(AXES, pos, off, sizes)}

    peers = offsets(sizes)

    load = pltpu.make_async_copy(state_hbm, st, load_sem)
    load.start()
    per = -(-S // CHUNKS)
    inv_loads = []
    for c in range(CHUNKS):
        lo, hi = c * per, min(S, (c + 1) * per)
        cp = pltpu.make_async_copy(inv_hbm.at[pl.ds(lo, hi - lo)], inv.at[pl.ds(lo, hi - lo)], inv_sem.at[c])
        cp.start()
        inv_loads.append(cp)

    barrier = pltpu.get_barrier_semaphore()
    lines = [[tuple(o if a == d else 0 for a in range(3)) for o in range(1, sizes[d])] for d in range(3)]
    near = lines[0] + lines[1] + lines[2]
    for off in near:
        pl.semaphore_signal(barrier, inc=1, device_id=at(off), device_id_type=MESH)

    def tell(i, line):
        for off in line:
            pl.semaphore_signal(ready.at[i], inc=1, device_id=at(off), device_id_type=MESH)

    row = lax.broadcasted_iota(jnp.int32, (8, L), 0)
    lane = lax.broadcasted_iota(jnp.int32, (8, L), 1)
    yy = lax.rem(row, 4)
    pp = lax.rem(lane, 4)
    f = lambda c: jnp.where(c, 1.0, 0.0).astype(jnp.float32)
    low_rows = f(row < 4)
    high_rows = f(row >= 4)

    def wall(d, edge):
        return jnp.where((bound_ref[d] == 0) & (pos[d] == edge), 1.0, 0.0).astype(jnp.float32)

    wx0, wx1 = wall(0, 0), wall(0, sizes[0] - 1)
    wy0, wy1 = wall(1, 0), wall(1, sizes[1] - 1)
    wz0, wz1 = wall(2, 0), wall(2, sizes[2] - 1)
    mx0, mx1, my0, my1, mz0, mz1 = [1.0 - w for w in (wx0, wx1, wy0, wy1, wz0, wz1)]

    rd = lambda ref, s, h: ref[s, pl.ds(8 * h, 8), :]

    grp = lane // 4

    def pack(field, k):
        def some(i, species):
            acc = jnp.zeros((8, L), jnp.float32)
            for g, s in enumerate(species):
                v0, v1 = rd(field, s, 0), rd(field, s, 1)
                ya[k, s] = jnp.where(yy < 2, pltpu.roll(v0, 6, 0), v1)
                yb[k, s] = jnp.where(yy < 2, v0, pltpu.roll(v1, 2, 0))
                acc = jnp.where(grp == 2 * g, pltpu.roll(v0, (8 * g + 2) % L, 1), acc)
                acc = jnp.where(grp == 2 * g + 1, pltpu.roll(v1, (8 * g + 6) % L, 1), acc)
            zp[k, tile8(i), :] = acc

        block_loop(some)

    def halo_copies(field, k):
        nx, ny, nz = sizes
        todo = [
            (field.at[:, pl.ds(8, 8), :], xlo.at[k], (1, 0, 0)),
            (field.at[:, pl.ds(0, 8), :], xhi.at[k], (nx - 1, 0, 0)),
            (zp.at[k], zlo.at[k], (0, 0, 1)),
            (zp.at[k], zhi.at[k], (0, 0, nz - 1)),
            (ya.at[k], yra.at[k], (0, 1, 0)),
            (yb.at[k], yrb.at[k], (0, ny - 1, 0)),
        ]
        cps = []
        for i, (src, dst, off) in enumerate(todo):
            cps.append(pltpu.make_async_remote_copy(
                src_ref=src, dst_ref=dst, send_sem=halo_send.at[k, i], recv_sem=halo_recv.at[k, i],
                device_id=at(off), device_id_type=MESH))
        return cps

    def inner(field, out):
        x0c = -30.0 + 16.0 * wx0 * low_rows
        x1c = -30.0 + 16.0 * wx1 * high_rows
        b1 = 16.0 * f(yy >= 1) - wy0 * f(yy == 1) - wy1 * f(yy == 3)
        bm1 = 16.0 * f(yy <= 2) - wy0 * f(yy == 0) - wy1 * f(yy == 2)
        b2, bm2 = -f(yy >= 2), -f(yy <= 1)
        a1 = 16.0 * f(lane >= 1) - wz0 * f(lane == 1) - wz1 * f(lane == L - 1)
        am1 = 16.0 * f(lane <= L - 2) - wz0 * f(lane == 0) - wz1 * f(lane == L - 2)
        a2, am2 = -f(lane >= 2), -f(lane <= L - 3)
        yz0 = (-60.0 + 16.0 * wy0 * f(yy == 0) + 16.0 * wy1 * f(yy == 3)
               + 16.0 * wz0 * f(lane == 0) + 16.0 * wz1 * f(lane == L - 1))
        own_drift = -DRIFT + DRIFT * wx0 * low_rows

        def one(s):
            c = diff_ref[s] * (1.0 / 12.0)
            v0, v1 = rd(field, s, 0), rd(field, s, 1)
            s0, s1 = pltpu.roll(v0, 4, 0), pltpu.roll(v1, 4, 0)

            def yz(v):
                return (yz0 * v + b1 * pltpu.roll(v, 1, 0) + b2 * pltpu.roll(v, 2, 0)
                        + bm1 * pltpu.roll(v, 7, 0) + bm2 * pltpu.roll(v, 6, 0)
                        + a1 * pltpu.roll(v, 1, 1) + a2 * pltpu.roll(v, 2, 1)
                        + am1 * pltpu.roll(v, L - 1, 1) + am2 * pltpu.roll(v, L - 2, 1))

            l0 = x0c * v0 + (16.0 - wx0) * s0 + 16.0 * high_rows * s1 - v1 + yz(v0)
            l1 = x1c * v1 + (16.0 - wx1) * s1 + 16.0 * low_rows * s0 - v0 + yz(v1)
            out[s, pl.ds(0, 8), :] = c * l0 + own_drift * v0 + DRIFT * high_rows * s0
            out[s, pl.ds(8, 8), :] = c * l1 - DRIFT * v1 + DRIFT * jnp.where(row >= 4, s1, s0)

        species_loop(one, 4)

    def outer(k, part, fin):
        edge = (lane < 2) | (lane >= L - 2)
        for q in range(4):
            lo = zlo[k, pl.ds(8 * q, 8), :]
            hi = zhi[k, pl.ds(8 * q, 8), :]
            from_hi = mz1 * (16.0 * f(pp == 1) * pltpu.roll(hi, L - 1, 1) - pltpu.roll(hi, L - 2, 1))
            from_lo = mz0 * (16.0 * f(pp == 2) * pltpu.roll(lo, 1, 1) - pltpu.roll(lo, 2, 1))
            zk[pl.ds(8 * q, 8), :] = jnp.where(pp < 2, from_hi, from_lo)
        even = 16.0 * my0 * f(lax.rem(row, 2) == 0)
        odd = 16.0 * my1 * f(lax.rem(row, 2) == 1)
        lo16, hi16, dr = 16.0 * mx0 * low_rows, 16.0 * mx1 * high_rows, DRIFT * mx0 * low_rows

        def some(i, species):
            zt = zk[tile8(i), :]
            for g, s in enumerate(species):
                c = diff_ref[s] * (1.0 / 12.0)
                xl, xh = xlo[k, s], xhi[k, s]
                a, b = yra[k, s], yrb[k, s]
                rl, rh = pltpu.roll(xl, 4, 0), pltpu.roll(xh, 4, 0)
                ca = even * pltpu.roll(a, 7, 0) - my0 * a
                cb = odd * pltpu.roll(b, 1, 0) - my1 * b
                z0 = pltpu.roll(zt, (2 * L - 2 - 8 * g) % L, 1)
                z1 = pltpu.roll(zt, (2 * L - 6 - 8 * g) % L, 1)
                l0 = lo16 * rl - mx0 * xl + jnp.where(yy < 2, ca, pltpu.roll(cb, 2, 0)) + jnp.where(edge, z0, 0.0)
                l1 = hi16 * rh - mx1 * xh + jnp.where(yy < 2, pltpu.roll(ca, 6, 0), cb) + jnp.where(edge, z1, 0.0)
                fin(s, 0, rd(part, s, 0) + c * l0 + dr * rl)
                fin(s, 1, rd(part, s, 1) + c * l1)

        block_loop(some)

    def put_tanh(s, h, v):
        start = s * R + 8 * h
        if not isinstance(s, int):
            start = pl.multiple_of(start, 8)
        tbuf[pl.ds(start, 8), :] = jnp.tanh(v)

    def chem_at(s, h):
        start = s * R + 8 * h
        if not isinstance(s, int):
            start = pl.multiple_of(start, 8)
        return cbuf[pl.ds(start, 8), :]

    def chemistry():
        lhs = rows_lhs()
        for r in range(0, R, 2):
            t = jnp.concatenate([tbuf[pl.ds(r + i, SP, stride=R), :] for i in range(2)], axis=1)
            hi = t.astype(jnp.bfloat16)
            lo = (t - hi.astype(jnp.float32)).astype(jnp.bfloat16)
            got = jnp.dot(lhs, jnp.concatenate([hi, lo, hi, lo], axis=0), preferred_element_type=jnp.float32)
            for i in range(2):
                cbuf[pl.ds(r + i, SP, stride=R), :] = got[:, i * L:(i + 1) * L]

    def rows_lhs():
        both = rpad[...] + pltpu.roll(rpad[...], SP, 1)
        hi = both.astype(jnp.bfloat16)
        lo = (both - hi.astype(jnp.float32)).astype(jnp.bfloat16)
        return jnp.concatenate([hi, lo], axis=1)

    def matvec():
        last = S - GROUP
        steps = -(-S // GROUP)
        again = steps * GROUP - S

        def columns(s0, j0, count, accs):
            accs = list(accs)
            for jj in range(count):
                g = gee[j0 + jj]
                for k in range(GROUP):
                    accs[k] = accs[k] + inv[s0 + k, j0 + jj] * g
            return tuple(accs)

        def body(i, total):
            s0 = jnp.minimum(i * GROUP, last)
            accs = tuple(jnp.zeros((R, L), jnp.float32) for _ in range(GROUP))
            accs = lax.fori_loop(0, S // JB, lambda t, acc: columns(s0, t * JB, JB, acc), accs)
            accs = columns(s0, S // JB * JB, S % JB, accs)
            fresh = jnp.where(i == steps - 1, 0.0, 1.0)
            for k in range(GROUP):
                dee[s0 + k] = accs[k]
                u = accs[k] * wts[s0 + k]
                u = u * u
                total = total + (u * fresh if k < again else u)
            return total

        return lax.fori_loop(0, steps, body, jnp.zeros((R, L), jnp.float32))

    def damping(k, total):
        rows[k, pl.ds(me, 1), :] = jnp.sum(total, axis=0, keepdims=True)
        for off in peers:
            pltpu.make_async_remote_copy(
                src_ref=rows.at[k, pl.ds(me, 1), :], dst_ref=rows.at[k, pl.ds(me, 1), :],
                send_sem=norm_send.at[k], recv_sem=norm_recv.at[k],
                device_id=at(off), device_id_type=MESH).start()
        all_rows(k).wait_recv()
        total = jnp.sum(jnp.sum(rows[k], axis=0, keepdims=True), axis=1, keepdims=True)
        return 1.0 / jnp.maximum(jnp.sqrt(total * (1.0 / entries)), 1.0)

    def all_rows(k):
        count = len(peers)
        return pltpu.make_async_remote_copy(
            src_ref=rows.at[k, pl.ds(0, count), :], dst_ref=rows.at[k, pl.ds(0, count), :],
            send_sem=norm_send.at[k], recv_sem=norm_recv.at[k],
            device_id=at(peers[0]), device_id_type=MESH)

    halves = [(0, pl.ds(0, 8)), (1, pl.ds(8, 8))]

    def newton(k, last):
        chemistry()

        def first(s):
            for h, hs in halves:
                gee[s, hs, :] = -GAMMA * chem_at(s, h)

        species_loop(first)
        if k == 0:
            for cp in inv_loads:
                cp.wait()
        total = matvec()
        if k == 0:
            pl.semaphore_wait(ready.at[1], len(lines[0]))
        r = damping(k, total)

        def mid(s):
            for h, hs in halves:
                z = base[s, hs, :] - dee[s, hs, :] * r
                zed[s, hs, :] = z
                put_tanh(s, h, z)

        species_loop(mid)
        chemistry()

        def second(s):
            for h, hs in halves:
                gee[s, hs, :] = zed[s, hs, :] - base[s, hs, :] - GAMMA * chem_at(s, h)

        species_loop(second)
        r2 = damping(k + 1, matvec())

        def end(s):
            for h, hs in halves:
                last(s, h, zed[s, hs, :] - dee[s, hs, :] * r2)

        species_loop(end)

    tbuf[pl.ds(S * R, (SP - S) * R), :] = jnp.zeros(((SP - S) * R, L), jnp.float32)
    rpad[...] = jnp.zeros((SP, L), jnp.float32)
    rpad[0:S, 0:S] = rates_ref[...]
    load.wait()
    pack(st, 0)
    pl.semaphore_wait(barrier, len(near))
    first_halo = halo_copies(st, 0)
    for cp in first_halo:
        cp.start()
    tell(0, lines[1])
    inner(st, e0)
    pl.semaphore_wait(ready.at[0], len(lines[1]))
    tell(1, lines[0])

    def weigh(s):
        wts[s] = 1.0 / (REL_TOL * jnp.abs(st[s]) + ABS_TOL)

    species_loop(weigh)
    for cp in first_halo:
        cp.wait_recv()

    def fin0(s, h, e):
        hs = pl.ds(8 * h, 8)
        e0[s, hs, :] = e
        b = st[s, hs, :] + GAMMA * e
        base[s, hs, :] = b
        put_tanh(s, h, b)

    outer(0, e0, fin0)

    def keep(s, h, v):
        sec[s, pl.ds(8 * h, 8), :] = v
        put_tanh(s, h, v)

    newton(0, keep)

    second_halo = halo_copies(sec, 1)
    for cp in second_halo[:2]:
        cp.start()
    pack(sec, 1)
    for cp in second_halo[2:]:
        cp.start()
    inner(sec, ebuf)
    chemistry()

    def pre(s):
        for h, hs in halves:
            base[s, hs, :] = st[s, hs, :] + DELTA * e0[s, hs, :] + (1.0 - GAMMA) * chem_at(s, h)

    species_loop(pre)
    for cp in second_halo:
        cp.wait_recv()

    def fin1(s, h, e):
        hs = pl.ds(8 * h, 8)
        b = base[s, hs, :] + (1.0 - DELTA) * e
        base[s, hs, :] = b
        put_tanh(s, h, b)

    outer(1, ebuf, fin1)

    def give(s, h, v):
        out_ref[s, pl.ds(8 * h, 8), :] = v

    newton(2, give)
    for cp in first_halo + second_halo:
        cp.wait_send()
    for k in range(4):
        all_rows(k).wait_send()


def body(sizes, state, diffusivity, rates, inverse, boundary):
    shape = state.shape
    field = pltpu.VMEM((S, R, L), jnp.float32)
    faces = pltpu.VMEM((2, S, 8, L), jnp.float32)
    n_all = sizes[0] * sizes[1] * sizes[2]
    out = pl.pallas_call(
        functools.partial(kernel, sizes),
        name="ark_step",
        out_shape=jax.ShapeDtypeStruct((S, R, L), jnp.float32),
        in_specs=[
            pl.BlockSpec(memory_space=pl.ANY),
            pl.BlockSpec(memory_space=pltpu.SMEM),
            pl.BlockSpec(memory_space=pltpu.VMEM),
            pl.BlockSpec(memory_space=pl.ANY),
            pl.BlockSpec(memory_space=pltpu.SMEM),
        ],
        out_specs=pl.BlockSpec(memory_space=pltpu.VMEM),
        scratch_shapes=[
            field, pltpu.VMEM((S, S, R, L), jnp.float32),
            faces, faces, faces, faces, faces, faces,
            pltpu.VMEM((2, 32, L), jnp.float32), pltpu.VMEM((32, L), jnp.float32),
            pltpu.VMEM((2, 32, L), jnp.float32), pltpu.VMEM((2, 32, L), jnp.float32),
            field, field, field, field, field, field, field, field,
            pltpu.VMEM((SP * R, L), jnp.float32), pltpu.VMEM((SP * R, L), jnp.float32),
            pltpu.VMEM((SP, L), jnp.float32), pltpu.VMEM((4, n_all, L), jnp.float32),
            pltpu.SemaphoreType.DMA, pltpu.SemaphoreType.DMA((CHUNKS,)),
            pltpu.SemaphoreType.DMA((2, 6)), pltpu.SemaphoreType.DMA((2, 6)),
            pltpu.SemaphoreType.DMA((4,)), pltpu.SemaphoreType.DMA((4,)), pltpu.SemaphoreType.REGULAR((2,)),
        ],
        compiler_params=pltpu.CompilerParams(collective_id=0, has_side_effects=True),
    )(
        state.reshape(S, R, L), diffusivity, rates, inverse.reshape(S, S, R, L), boundary,
    )
    return out.reshape(shape)


def solution(mesh):
    sizes = tuple(mesh.shape[a] for a in AXES)
    in_specs = (P(None, "gx", "gy", "gz"), P(), P(), P(None, None, "gx", "gy", "gz"), P())
    return jax.shard_map(
        functools.partial(body, sizes), mesh=mesh, in_specs=in_specs, out_specs=P(None, "gx", "gy", "gz"), check_vma=False)
```

```python
import functools
import itertools

import jax
import jax.numpy as jnp
from jax import lax
from jax.experimental import pallas as pl
from jax.experimental.pallas import tpu as pltpu
from jax.sharding import PartitionSpec as P

MESH = pl.DeviceIdType.MESH
AXES = ("gx", "gy", "gz")

GAMMA = 0.2928932188134524
DELTA = -0.7071067811865475
REL_TOL = 0.1
ABS_TOL = 0.05
DRIFT = 0.2

S = 53
SP = 64
R = 16
L = 128
GROUP = 18
JB = 8
CHUNKS = 8


def offsets(sizes):
    out = []
    for off in itertools.product(*[range(n) for n in sizes]):
        if any(off):
            out.append(off)

    def hops(off):
        gx, gy, gz = off
        ring = lambda d, n: min(d % n, n - d % n)
        far_y = ring(gy, sizes[1])
        far_z = ring(gx // 2, sizes[0] // 2)
        far_x = ring(2 * (gx % 2) + gz // 2, 4)
        return far_x + far_y + far_z

    return sorted(out, key=lambda off: -hops(off))


def species_loop(fn, block=4):
    whole = S // block

    def body(i, carry):
        for k in range(block):
            fn(i * block + k)
        return carry

    lax.fori_loop(0, whole, body, 0)
    for s in range(whole * block, S):
        fn(s)


def block_loop(fn, block=16):
    whole = S // block

    def body(i, carry):
        fn(i, [i * block + k for k in range(block)])
        return carry

    lax.fori_loop(0, whole, body, 0)
    fn(whole, list(range(whole * block, S)))


def tile8(i):
    return pl.ds(8 * i if isinstance(i, int) else pl.multiple_of(8 * i, 8), 8)


def kernel(
    sizes,
    state_hbm, diff_hbm, rates_hbm, inv_hbm, bound_hbm,
    out_ref,
    diff_ref, rates_ref, bound_ref, st, inv, xlo, xhi, ya, yb, yra, yrb, zp, zk, zlo, zhi,
    e0, ebuf, wts, base, zed, sec, dee, gee, tbuf, cbuf, rpad, rows,
    load_sem, inv_sem, halo_send, halo_recv, norm_send, norm_recv, ready,
):
    n_all = sizes[0] * sizes[1] * sizes[2]
    entries = float(S * R * L * n_all)
    pos = [lax.axis_index(a) for a in AXES]
    me = (pos[0] * sizes[1] + pos[1]) * sizes[2] + pos[2]

    def at(off):
        return {a: lax.rem(p + o, n) for a, p, o, n in zip(AXES, pos, off, sizes)}

    peers = offsets(sizes)

    barrier = pltpu.get_barrier_semaphore()
    lines = [[tuple(o if a == d else 0 for a in range(3)) for o in range(1, sizes[d])] for d in range(3)]
    near = lines[0] + lines[1] + lines[2]
    for off in near:
        pl.semaphore_signal(barrier, inc=1, device_id=at(off), device_id_type=MESH)

    load = pltpu.make_async_copy(state_hbm, st, load_sem.at[0])
    load.start()
    small = [pltpu.make_async_copy(src, dst, load_sem.at[i]) for i, (src, dst) in enumerate(
        [(diff_hbm, diff_ref), (rates_hbm, rates_ref), (bound_hbm, bound_ref)], 1)]
    for cp in small:
        cp.start()
    per = -(-S // CHUNKS)
    inv_loads = []
    for c in range(CHUNKS):
        lo, hi = c * per, min(S, (c + 1) * per)
        cp = pltpu.make_async_copy(inv_hbm.at[pl.ds(lo, hi - lo)], inv.at[pl.ds(lo, hi - lo)], inv_sem.at[c])
        cp.start()
        inv_loads.append(cp)

    def tell(i, line):
        for off in line:
            pl.semaphore_signal(ready.at[i], inc=1, device_id=at(off), device_id_type=MESH)

    for cp in small:
        cp.wait()

    row = lax.broadcasted_iota(jnp.int32, (8, L), 0)
    lane = lax.broadcasted_iota(jnp.int32, (8, L), 1)
    yy = lax.rem(row, 4)
    pp = lax.rem(lane, 4)
    f = lambda c: jnp.where(c, 1.0, 0.0).astype(jnp.float32)
    low_rows = f(row < 4)
    high_rows = f(row >= 4)

    def wall(d, edge):
        return jnp.where((bound_ref[d] == 0) & (pos[d] == edge), 1.0, 0.0).astype(jnp.float32)

    wx0, wx1 = wall(0, 0), wall(0, sizes[0] - 1)
    wy0, wy1 = wall(1, 0), wall(1, sizes[1] - 1)
    wz0, wz1 = wall(2, 0), wall(2, sizes[2] - 1)
    mx0, mx1, my0, my1, mz0, mz1 = [1.0 - w for w in (wx0, wx1, wy0, wy1, wz0, wz1)]

    rd = lambda ref, s, h: ref[s, pl.ds(8 * h, 8), :]

    grp = lane // 4

    def pack(field, k):
        def some(i, species):
            acc = jnp.zeros((8, L), jnp.float32)
            for g, s in enumerate(species):
                v0, v1 = rd(field, s, 0), rd(field, s, 1)
                ya[k, s] = jnp.where(yy < 2, pltpu.roll(v0, 6, 0), v1)
                yb[k, s] = jnp.where(yy < 2, v0, pltpu.roll(v1, 2, 0))
                acc = jnp.where(grp == 2 * g, pltpu.roll(v0, (8 * g + 2) % L, 1), acc)
                acc = jnp.where(grp == 2 * g + 1, pltpu.roll(v1, (8 * g + 6) % L, 1), acc)
            zp[k, tile8(i), :] = acc

        block_loop(some)

    def halo_copies(field, k):
        nx, ny, nz = sizes
        todo = [
            (field.at[:, pl.ds(8, 8), :], xlo.at[k], (1, 0, 0)),
            (field.at[:, pl.ds(0, 8), :], xhi.at[k], (nx - 1, 0, 0)),
            (zp.at[k], zlo.at[k], (0, 0, 1)),
            (zp.at[k], zhi.at[k], (0, 0, nz - 1)),
            (ya.at[k], yra.at[k], (0, 1, 0)),
            (yb.at[k], yrb.at[k], (0, ny - 1, 0)),
        ]
        cps = []
        for i, (src, dst, off) in enumerate(todo):
            cps.append(pltpu.make_async_remote_copy(
                src_ref=src, dst_ref=dst, send_sem=halo_send.at[k, i], recv_sem=halo_recv.at[k, i],
                device_id=at(off), device_id_type=MESH))
        return cps

    def inner(field, out):
        x0c = -30.0 + 16.0 * wx0 * low_rows
        x1c = -30.0 + 16.0 * wx1 * high_rows
        b1 = 16.0 * f(yy >= 1) - wy0 * f(yy == 1) - wy1 * f(yy == 3)
        bm1 = 16.0 * f(yy <= 2) - wy0 * f(yy == 0) - wy1 * f(yy == 2)
        b2, bm2 = -f(yy >= 2), -f(yy <= 1)
        a1 = 16.0 * f(lane >= 1) - wz0 * f(lane == 1) - wz1 * f(lane == L - 1)
        am1 = 16.0 * f(lane <= L - 2) - wz0 * f(lane == 0) - wz1 * f(lane == L - 2)
        a2, am2 = -f(lane >= 2), -f(lane <= L - 3)
        yz0 = (-60.0 + 16.0 * wy0 * f(yy == 0) + 16.0 * wy1 * f(yy == 3)
               + 16.0 * wz0 * f(lane == 0) + 16.0 * wz1 * f(lane == L - 1))
        own_drift = -DRIFT + DRIFT * wx0 * low_rows

        def one(s):
            c = diff_ref[s] * (1.0 / 12.0)
            v0, v1 = rd(field, s, 0), rd(field, s, 1)
            s0, s1 = pltpu.roll(v0, 4, 0), pltpu.roll(v1, 4, 0)

            def yz(v):
                return (yz0 * v + b1 * pltpu.roll(v, 1, 0) + b2 * pltpu.roll(v, 2, 0)
                        + bm1 * pltpu.roll(v, 7, 0) + bm2 * pltpu.roll(v, 6, 0)
                        + a1 * pltpu.roll(v, 1, 1) + a2 * pltpu.roll(v, 2, 1)
                        + am1 * pltpu.roll(v, L - 1, 1) + am2 * pltpu.roll(v, L - 2, 1))

            l0 = x0c * v0 + (16.0 - wx0) * s0 + 16.0 * high_rows * s1 - v1 + yz(v0)
            l1 = x1c * v1 + (16.0 - wx1) * s1 + 16.0 * low_rows * s0 - v0 + yz(v1)
            out[s, pl.ds(0, 8), :] = c * l0 + own_drift * v0 + DRIFT * high_rows * s0
            out[s, pl.ds(8, 8), :] = c * l1 - DRIFT * v1 + DRIFT * jnp.where(row >= 4, s1, s0)

        species_loop(one, 4)

    def outer_z(k):
        for q in range(4):
            lo = zlo[k, pl.ds(8 * q, 8), :]
            hi = zhi[k, pl.ds(8 * q, 8), :]
            from_hi = mz1 * (16.0 * f(pp == 1) * pltpu.roll(hi, L - 1, 1) - pltpu.roll(hi, L - 2, 1))
            from_lo = mz0 * (16.0 * f(pp == 2) * pltpu.roll(lo, 1, 1) - pltpu.roll(lo, 2, 1))
            zk[pl.ds(8 * q, 8), :] = jnp.where(pp < 2, from_hi, from_lo)

    def outer(k, h, part, fin):
        edge = (lane < 2) | (lane >= L - 2)
        even = 16.0 * my0 * f(lax.rem(row, 2) == 0)
        odd = 16.0 * my1 * f(lax.rem(row, 2) == 1)
        lo16, hi16, dr = 16.0 * mx0 * low_rows, 16.0 * mx1 * high_rows, DRIFT * mx0 * low_rows

        def some(i, species):
            zt = zk[tile8(i), :]
            for g, s in enumerate(species):
                c = diff_ref[s] * (1.0 / 12.0)
                a, b = yra[k, s], yrb[k, s]
                ca = even * pltpu.roll(a, 7, 0) - my0 * a
                cb = odd * pltpu.roll(b, 1, 0) - my1 * b
                z = jnp.where(edge, pltpu.roll(zt, (2 * L - 2 - 8 * g - 4 * h) % L, 1), 0.0)
                if h == 0:
                    x = xlo[k, s]
                    turned = pltpu.roll(x, 4, 0)
                    lap = lo16 * turned - mx0 * x + jnp.where(yy < 2, ca, pltpu.roll(cb, 2, 0)) + z
                    fin(s, h, rd(part, s, h) + c * lap + dr * turned)
                else:
                    x = xhi[k, s]
                    lap = hi16 * pltpu.roll(x, 4, 0) - mx1 * x + jnp.where(yy < 2, pltpu.roll(ca, 6, 0), cb) + z
                    fin(s, h, rd(part, s, h) + c * lap)

        block_loop(some)

    def put_tanh(s, h, v):
        start = s * R + 8 * h
        if not isinstance(s, int):
            start = pl.multiple_of(start, 8)
        tbuf[pl.ds(start, 8), :] = jnp.tanh(v)

    def chem_at(s, h):
        start = s * R + 8 * h
        if not isinstance(s, int):
            start = pl.multiple_of(start, 8)
        return cbuf[pl.ds(start, 8), :]

    def chemistry(first=0, rows_done=R):
        lhs = rows_lhs()
        for r in range(first, first + rows_done, 2):
            t = jnp.concatenate([tbuf[pl.ds(r + i, SP, stride=R), :] for i in range(2)], axis=1)
            hi = t.astype(jnp.bfloat16)
            lo = (t - hi.astype(jnp.float32)).astype(jnp.bfloat16)
            got = jnp.dot(lhs, jnp.concatenate([hi, lo, hi, lo], axis=0), preferred_element_type=jnp.float32)
            for i in range(2):
                cbuf[pl.ds(r + i, SP, stride=R), :] = got[:, i * L:(i + 1) * L]

    def rows_lhs():
        both = rpad[...] + pltpu.roll(rpad[...], SP, 1)
        hi = both.astype(jnp.bfloat16)
        lo = (both - hi.astype(jnp.float32)).astype(jnp.bfloat16)
        return jnp.concatenate([hi, lo], axis=1)

    def matvec(h, total):
        last = S - GROUP
        steps = -(-S // GROUP)
        again = steps * GROUP - S
        hs = pl.ds(8 * h, 8)

        def columns(s0, j0, count, accs):
            accs = list(accs)
            for jj in range(count):
                g = gee[j0 + jj, hs, :]
                for k in range(GROUP):
                    accs[k] = accs[k] + inv[s0 + k, j0 + jj, hs, :] * g
            return tuple(accs)

        def body(i, total):
            s0 = jnp.minimum(i * GROUP, last)
            accs = tuple(jnp.zeros((8, L), jnp.float32) for _ in range(GROUP))
            accs = lax.fori_loop(0, S // JB, lambda t, acc: columns(s0, t * JB, JB, acc), accs)
            accs = columns(s0, S // JB * JB, S % JB, accs)
            fresh = jnp.where(i == steps - 1, 0.0, 1.0)
            for k in range(GROUP):
                dee[s0 + k, hs, :] = accs[k]
                u = accs[k] * wts[s0 + k, hs, :]
                u = u * u
                total = total + (u * fresh if k < again else u)
            return total

        return lax.fori_loop(0, steps, body, total)

    def damping(k, total):
        rows[k, pl.ds(me, 1), :] = jnp.sum(total, axis=0, keepdims=True)
        for off in peers:
            pltpu.make_async_remote_copy(
                src_ref=rows.at[k, pl.ds(me, 1), :], dst_ref=rows.at[k, pl.ds(me, 1), :],
                send_sem=norm_send.at[k], recv_sem=norm_recv.at[k],
                device_id=at(off), device_id_type=MESH).start()
        all_rows(k).wait_recv()
        total = jnp.sum(jnp.sum(rows[k], axis=0, keepdims=True), axis=1, keepdims=True)
        return 1.0 / jnp.maximum(jnp.sqrt(total * (1.0 / entries)), 1.0)

    def all_rows(k):
        count = len(peers)
        return pltpu.make_async_remote_copy(
            src_ref=rows.at[k, pl.ds(0, count), :], dst_ref=rows.at[k, pl.ds(0, count), :],
            send_sem=norm_send.at[k], recv_sem=norm_recv.at[k],
            device_id=at(peers[0]), device_id_type=MESH)

    halves = [(0, pl.ds(0, 8)), (1, pl.ds(8, 8))]

    def newton(k, last, faces):
        total = jnp.zeros((8, L), jnp.float32)
        for h, hs in halves:
            faces(h)
            chemistry(8 * h, 8)

            def first(s):
                gee[s, hs, :] = -GAMMA * chem_at(s, h)

            species_loop(first)
            if k == 0 and h == 0:
                for cp in inv_loads:
                    cp.wait()
            total = matvec(h, total)
        if k == 0:
            pl.semaphore_wait(ready.at[1], len(lines[0]))
        r = damping(k, total)

        def mid(s):
            for h, hs in halves:
                z = base[s, hs, :] - dee[s, hs, :] * r
                zed[s, hs, :] = z
                put_tanh(s, h, z)

        species_loop(mid)
        chemistry()

        def second(s):
            for h, hs in halves:
                gee[s, hs, :] = zed[s, hs, :] - base[s, hs, :] - GAMMA * chem_at(s, h)

        species_loop(second)
        r2 = damping(k + 1, matvec(1, matvec(0, jnp.zeros((8, L), jnp.float32))))

        def end(s):
            for h, hs in halves:
                last(s, h, zed[s, hs, :] - dee[s, hs, :] * r2)

        species_loop(end)

    tbuf[pl.ds(S * R, (SP - S) * R), :] = jnp.zeros(((SP - S) * R, L), jnp.float32)
    rpad[...] = jnp.zeros((SP, L), jnp.float32)
    rpad[0:S, 0:S] = rates_ref[...]
    load.wait()
    pack(st, 0)
    pl.semaphore_wait(barrier, len(near))
    first_halo = halo_copies(st, 0)
    for cp in first_halo[:1] + first_halo[2:]:
        cp.start()
    tell(0, lines[1])
    inner(st, e0)
    pl.semaphore_wait(ready.at[0], len(lines[1]))
    tell(1, lines[0])

    def weigh(s):
        wts[s] = 1.0 / (REL_TOL * jnp.abs(st[s]) + ABS_TOL)

    species_loop(weigh)
    first_halo[0].wait_send()
    first_halo[1].start()

    def fin0(s, h, e):
        hs = pl.ds(8 * h, 8)
        e0[s, hs, :] = e
        b = st[s, hs, :] + GAMMA * e
        base[s, hs, :] = b
        put_tanh(s, h, b)

    def faces0(h):
        if h == 0:
            for cp in first_halo[:1] + first_halo[2:]:
                cp.wait_recv()
            outer_z(0)
        else:
            first_halo[1].wait_recv()
        outer(0, h, e0, fin0)

    def keep(s, h, v):
        sec[s, pl.ds(8 * h, 8), :] = v
        put_tanh(s, h, v)

    newton(0, keep, faces0)

    second_halo = halo_copies(sec, 1)
    second_halo[0].start()
    pack(sec, 1)
    for cp in second_halo[2:]:
        cp.start()
    inner(sec, ebuf)
    chemistry()

    def pre(s):
        for h, hs in halves:
            base[s, hs, :] = st[s, hs, :] + DELTA * e0[s, hs, :] + (1.0 - GAMMA) * chem_at(s, h)

    species_loop(pre)
    second_halo[0].wait_send()
    second_halo[1].start()

    def fin1(s, h, e):
        hs = pl.ds(8 * h, 8)
        b = base[s, hs, :] + (1.0 - DELTA) * e
        base[s, hs, :] = b
        put_tanh(s, h, b)

    def faces1(h):
        if h == 0:
            for cp in second_halo[:1] + second_halo[2:]:
                cp.wait_recv()
            outer_z(1)
        else:
            second_halo[1].wait_recv()
        outer(1, h, ebuf, fin1)

    def give(s, h, v):
        out_ref[s, pl.ds(8 * h, 8), :] = v

    newton(2, give, faces1)
    for cp in first_halo[1:] + second_halo[1:]:
        cp.wait_send()
    for k in range(4):
        all_rows(k).wait_send()


def body(sizes, state, diffusivity, rates, inverse, boundary):
    shape = state.shape
    field = pltpu.VMEM((S, R, L), jnp.float32)
    faces = pltpu.VMEM((2, S, 8, L), jnp.float32)
    n_all = sizes[0] * sizes[1] * sizes[2]
    out = pl.pallas_call(
        functools.partial(kernel, sizes),
        name="ark_step",
        out_shape=jax.ShapeDtypeStruct((S, R, L), jnp.float32),
        in_specs=[
            pl.BlockSpec(memory_space=pltpu.HBM) for _ in range(5)
        ],
        out_specs=pl.BlockSpec(memory_space=pltpu.VMEM),
        scratch_shapes=[
            pltpu.SMEM((S,), jnp.float32), pltpu.VMEM((S, S), jnp.float32), pltpu.SMEM((3,), jnp.int32),
            field, pltpu.VMEM((S, S, R, L), jnp.float32),
            faces, faces, faces, faces, faces, faces,
            pltpu.VMEM((2, 32, L), jnp.float32), pltpu.VMEM((32, L), jnp.float32),
            pltpu.VMEM((2, 32, L), jnp.float32), pltpu.VMEM((2, 32, L), jnp.float32),
            field, field, field, field, field, field, field, field,
            pltpu.VMEM((SP * R, L), jnp.float32), pltpu.VMEM((SP * R, L), jnp.float32),
            pltpu.VMEM((SP, L), jnp.float32), pltpu.VMEM((4, n_all, L), jnp.float32),
            pltpu.SemaphoreType.DMA((4,)), pltpu.SemaphoreType.DMA((CHUNKS,)),
            pltpu.SemaphoreType.DMA((2, 6)), pltpu.SemaphoreType.DMA((2, 6)),
            pltpu.SemaphoreType.DMA((4,)), pltpu.SemaphoreType.DMA((4,)), pltpu.SemaphoreType.REGULAR((2,)),
        ],
        compiler_params=pltpu.CompilerParams(collective_id=0, has_side_effects=True, vmem_limit_bytes=48 << 20),
    )(
        *[pltpu.with_memory_space_constraint(a, pltpu.HBM) for a in (
            state.reshape(S, R, L), diffusivity, rates, inverse.reshape(S, S, R, L), boundary)],
    )
    return out.reshape(shape)


def solution(mesh):
    sizes = tuple(mesh.shape[a] for a in AXES)
    in_specs = (P(None, "gx", "gy", "gz"), P(), P(), P(None, None, "gx", "gy", "gz"), P())
    return jax.shard_map(
        functools.partial(body, sizes), mesh=mesh, in_specs=in_specs, out_specs=P(None, "gx", "gy", "gz"), check_vma=False)
```

```python
import functools
import itertools

import jax
import jax.numpy as jnp
from jax import lax
from jax.experimental import pallas as pl
from jax.experimental.pallas import tpu as pltpu
from jax.sharding import PartitionSpec as P

MESH = pl.DeviceIdType.MESH
AXES = ("gx", "gy", "gz")

GAMMA = 0.2928932188134524
DELTA = -0.7071067811865475
REL_TOL = 0.1
ABS_TOL = 0.05
DRIFT = 0.2

S = 53
SP = 64
R = 16
L = 128
GROUP = 18
JB = 8
EARLY = 17
CHUNKS = 8


def offsets(sizes):
    out = []
    for off in itertools.product(*[range(n) for n in sizes]):
        if any(off):
            out.append(off)

    def hops(off):
        gx, gy, gz = off
        ring = lambda d, n: min(d % n, n - d % n)
        far_y = ring(gy, sizes[1])
        far_z = ring(gx // 2, sizes[0] // 2)
        far_x = ring(2 * (gx % 2) + gz // 2, 4)
        return far_x + far_y + far_z

    return sorted(out, key=lambda off: -hops(off))


def species_loop(fn, block=8):
    whole = S // block

    def body(i, carry):
        for k in range(block):
            fn(i * block + k)
        return carry

    lax.fori_loop(0, whole, body, 0)
    for s in range(whole * block, S):
        fn(s)


def block_loop(fn, block=16, unroll=False):
    whole = S // block
    if unroll:
        for i in range(whole + 1):
            fn(i, list(range(i * block, min(S, (i + 1) * block))))
        return

    def body(i, carry):
        fn(i, [i * block + k for k in range(block)])
        return carry

    lax.fori_loop(0, whole, body, 0)
    fn(whole, list(range(whole * block, S)))


def tile8(i):
    return pl.ds(8 * i if isinstance(i, int) else pl.multiple_of(8 * i, 8), 8)


def kernel(
    sizes,
    state_hbm, diff_hbm, rates_hbm, inv_hbm, bound_hbm,
    out_ref,
    diff_ref, rates_ref, bound_ref, st, inv, xlo, xhi, dlo, dhi, ya, yb, yra, yrb, zp, zk, zlo, zhi,
    e0, ebuf, wts, base, zed, sec, dee, tbuf, cbuf, rpad, rows,
    load_sem, inv_sem, halo_send, halo_recv, early_send, early_recv, norm_send, norm_recv, ready,
):
    n_all = sizes[0] * sizes[1] * sizes[2]
    entries = float(S * R * L * n_all)
    pos = [lax.axis_index(a) for a in AXES]
    me = (pos[0] * sizes[1] + pos[1]) * sizes[2] + pos[2]

    def at(off):
        return {a: lax.rem(p + o, n) for a, p, o, n in zip(AXES, pos, off, sizes)}

    peers = offsets(sizes)

    ahead = [(1, 0, 0), (0, 1, 0), (0, 0, 1)]
    back = [tuple((sizes[d] - 1) * o for d, o in enumerate(off)) for off in ahead]

    barrier = pltpu.get_barrier_semaphore()
    lines = [[tuple(o if a == d else 0 for a in range(3)) for o in range(1, sizes[d])] for d in range(3)]
    near = lines[0] + lines[1] + lines[2]
    for off in ahead[:1] + back[:1] + [o for o in near if o not in (ahead[0], back[0])]:
        pl.semaphore_signal(barrier, inc=1, device_id=at(off), device_id_type=MESH)

    load = pltpu.make_async_copy(state_hbm, st, load_sem.at[0])
    load.start()
    small = [pltpu.make_async_copy(src, dst, load_sem.at[i]) for i, (src, dst) in enumerate(
        [(diff_hbm, diff_ref), (rates_hbm, rates_ref), (bound_hbm, bound_ref)], 1)]
    for cp in small:
        cp.start()
    per = -(-S // CHUNKS)
    inv_loads = []
    for c in range(CHUNKS):
        lo, hi = c * per, min(S, (c + 1) * per)
        cp = pltpu.make_async_copy(inv_hbm.at[pl.ds(lo, hi - lo)], inv.at[pl.ds(lo, hi - lo)], inv_sem.at[c])
        cp.start()
        inv_loads.append(cp)

    def tell(i, line):
        for off in line:
            pl.semaphore_signal(ready.at[i], inc=1, device_id=at(off), device_id_type=MESH)

    for cp in small:
        cp.wait()

    row = lax.broadcasted_iota(jnp.int32, (8, L), 0)
    lane = lax.broadcasted_iota(jnp.int32, (8, L), 1)
    yy = lax.rem(row, 4)
    pp = lax.rem(lane, 4)
    f = lambda c: jnp.where(c, 1.0, 0.0).astype(jnp.float32)
    low_rows = f(row < 4)
    high_rows = f(row >= 4)

    def wall(d, edge):
        return jnp.where((bound_ref[d] == 0) & (pos[d] == edge), 1.0, 0.0).astype(jnp.float32)

    wx0, wx1 = wall(0, 0), wall(0, sizes[0] - 1)
    wy0, wy1 = wall(1, 0), wall(1, sizes[1] - 1)
    wz0, wz1 = wall(2, 0), wall(2, sizes[2] - 1)
    mx0, mx1, my0, my1, mz0, mz1 = [1.0 - w for w in (wx0, wx1, wy0, wy1, wz0, wz1)]

    rd = lambda ref, s, h: ref[s, pl.ds(8 * h, 8), :]

    grp = lane // 4

    def pack(field, k):
        def some(i, species):
            acc = jnp.zeros((8, L), jnp.float32)
            for g, s in enumerate(species):
                v0, v1 = rd(field, s, 0), rd(field, s, 1)
                ya[k, s] = jnp.where(yy < 2, pltpu.roll(v0, 6, 0), v1)
                yb[k, s] = jnp.where(yy < 2, v0, pltpu.roll(v1, 2, 0))
                acc = jnp.where(grp == 2 * g, pltpu.roll(v0, (8 * g + 2) % L, 1), acc)
                acc = jnp.where(grp == 2 * g + 1, pltpu.roll(v1, (8 * g + 6) % L, 1), acc)
            zp[k, tile8(i), :] = acc

        block_loop(some)

    def remote(src, dst, off, send, recv):
        return pltpu.make_async_remote_copy(
            src_ref=src, dst_ref=dst, send_sem=send, recv_sem=recv, device_id=at(off), device_id_type=MESH)

    def x_pair(field, first, count, lo, hi, sends, recvs, i):
        some = pl.ds(first, count)
        return [
            remote(field.at[some, pl.ds(8, 8), :], lo.at[some], ahead[0], sends.at[i], recvs.at[i]),
            remote(field.at[some, pl.ds(0, 8), :], hi.at[some], back[0], sends.at[i + 1], recvs.at[i + 1]),
        ]

    def halo_copies(field, k, first):
        todo = [
            (zp.at[k], zlo.at[k], ahead[2]),
            (zp.at[k], zhi.at[k], back[2]),
            (ya.at[k], yra.at[k], ahead[1]),
            (yb.at[k], yrb.at[k], back[1]),
        ]
        cps = x_pair(field, first, S - first, xlo.at[k], xhi.at[k], halo_send.at[k], halo_recv.at[k], 0)
        for i, (src, dst, off) in enumerate(todo, 2):
            cps.append(remote(src, dst, off, halo_send.at[k, i], halo_recv.at[k, i]))
        return cps

    def inner(field, out):
        x0c = -30.0 + 16.0 * wx0 * low_rows
        x1c = -30.0 + 16.0 * wx1 * high_rows
        b1 = 16.0 * f(yy >= 1) - wy0 * f(yy == 1) - wy1 * f(yy == 3)
        bm1 = 16.0 * f(yy <= 2) - wy0 * f(yy == 0) - wy1 * f(yy == 2)
        b2, bm2 = -f(yy >= 2), -f(yy <= 1)
        a1 = 16.0 * f(lane >= 1) - wz0 * f(lane == 1) - wz1 * f(lane == L - 1)
        am1 = 16.0 * f(lane <= L - 2) - wz0 * f(lane == 0) - wz1 * f(lane == L - 2)
        a2, am2 = -f(lane >= 2), -f(lane <= L - 3)
        yz0 = (-60.0 + 16.0 * wy0 * f(yy == 0) + 16.0 * wy1 * f(yy == 3)
               + 16.0 * wz0 * f(lane == 0) + 16.0 * wz1 * f(lane == L - 1))
        own_drift = -DRIFT + DRIFT * wx0 * low_rows

        def one(s):
            c = diff_ref[s] * (1.0 / 12.0)
            v0, v1 = rd(field, s, 0), rd(field, s, 1)
            s0, s1 = pltpu.roll(v0, 4, 0), pltpu.roll(v1, 4, 0)

            def yz(v):
                return (yz0 * v + b1 * pltpu.roll(v, 1, 0) + b2 * pltpu.roll(v, 2, 0)
                        + bm1 * pltpu.roll(v, 7, 0) + bm2 * pltpu.roll(v, 6, 0)
                        + a1 * pltpu.roll(v, 1, 1) + a2 * pltpu.roll(v, 2, 1)
                        + am1 * pltpu.roll(v, L - 1, 1) + am2 * pltpu.roll(v, L - 2, 1))

            l0 = x0c * v0 + (16.0 - wx0) * s0 + 16.0 * high_rows * s1 - v1 + yz(v0)
            l1 = x1c * v1 + (16.0 - wx1) * s1 + 16.0 * low_rows * s0 - v0 + yz(v1)
            out[s, pl.ds(0, 8), :] = c * l0 + own_drift * v0 + DRIFT * high_rows * s0
            out[s, pl.ds(8, 8), :] = c * l1 - DRIFT * v1 + DRIFT * jnp.where(row >= 4, s1, s0)

        species_loop(one, 4)

    def outer_z(k):
        for q in range(4):
            lo = zlo[k, pl.ds(8 * q, 8), :]
            hi = zhi[k, pl.ds(8 * q, 8), :]
            from_hi = mz1 * (16.0 * f(pp == 1) * pltpu.roll(hi, L - 1, 1) - pltpu.roll(hi, L - 2, 1))
            from_lo = mz0 * (16.0 * f(pp == 2) * pltpu.roll(lo, 1, 1) - pltpu.roll(lo, 2, 1))
            zk[pl.ds(8 * q, 8), :] = jnp.where(pp < 2, from_hi, from_lo)

    def outer(k, h, part, fin, r=None):
        edge = (lane < 2) | (lane >= L - 2)
        even = 16.0 * my0 * f(lax.rem(row, 2) == 0)
        odd = 16.0 * my1 * f(lax.rem(row, 2) == 1)
        lo16, hi16, dr = 16.0 * mx0 * low_rows, 16.0 * mx1 * high_rows, DRIFT * mx0 * low_rows

        def some(i, species):
            zt = zk[tile8(i), :]
            for g, s in enumerate(species):
                c = diff_ref[s] * (1.0 / 12.0)
                a, b = yra[k, s], yrb[k, s]
                ca = even * pltpu.roll(a, 7, 0) - my0 * a
                cb = odd * pltpu.roll(b, 1, 0) - my1 * b
                z = jnp.where(edge, pltpu.roll(zt, (2 * L - 2 - 8 * g - 4 * h) % L, 1), 0.0)
                if h == 0:
                    x = xlo[k, s]
                    if r is not None and s < EARLY:
                        x = x - dlo[s] * r
                    turned = pltpu.roll(x, 4, 0)
                    lap = lo16 * turned - mx0 * x + jnp.where(yy < 2, ca, pltpu.roll(cb, 2, 0)) + z
                    fin(s, h, rd(part, s, h) + c * lap + dr * turned)
                else:
                    x = xhi[k, s]
                    if r is not None and s < EARLY:
                        x = x - dhi[s] * r
                    lap = hi16 * pltpu.roll(x, 4, 0) - mx1 * x + jnp.where(yy < 2, pltpu.roll(ca, 6, 0), cb) + z
                    fin(s, h, rd(part, s, h) + c * lap)

        block_loop(some, unroll=r is not None)

    def cell_rows(s, h):
        start = s * R + 8 * h
        return pl.ds(start if isinstance(start, int) else pl.multiple_of(start, 8), 8)

    def put_tanh(s, h, v):
        tbuf[cell_rows(s, h), :] = jnp.tanh(v)

    def chemistry(first=0, rows_done=R):
        lhs = rows_lhs()
        for r in range(first, first + rows_done, 2):
            t = jnp.concatenate([tbuf[pl.ds(r + i, SP, stride=R), :] for i in range(2)], axis=1)
            hi = t.astype(jnp.bfloat16)
            lo = (t - hi.astype(jnp.float32)).astype(jnp.bfloat16)
            got = jnp.dot(lhs, jnp.concatenate([hi, lo, hi, lo], axis=0), preferred_element_type=jnp.float32)
            for i in range(2):
                cbuf[pl.ds(r + i, SP, stride=R), :] = got[:, i * L:(i + 1) * L]

    def rows_lhs():
        both = rpad[...] + pltpu.roll(rpad[...], SP, 1)
        hi = both.astype(jnp.bfloat16)
        lo = (both - hi.astype(jnp.float32)).astype(jnp.bfloat16)
        return jnp.concatenate([hi, lo], axis=1)

    def matvec(h, total):
        last = S - GROUP
        steps = -(-S // GROUP)
        again = steps * GROUP - S
        hs = pl.ds(8 * h, 8)

        def columns(s0, j0, count, accs):
            accs = list(accs)
            for jj in range(count):
                g = cbuf[cell_rows(j0 + jj, h), :]
                for k in range(GROUP):
                    accs[k] = accs[k] + inv[s0 + k, j0 + jj, hs, :] * g
            return tuple(accs)

        def body(i, total):
            s0 = jnp.minimum(i * GROUP, last)
            accs = tuple(jnp.zeros((8, L), jnp.float32) for _ in range(GROUP))
            accs = lax.fori_loop(0, S // JB, lambda t, acc: columns(s0, t * JB, JB, acc), accs)
            accs = columns(s0, S // JB * JB, S % JB, accs)
            fresh = jnp.where(i == steps - 1, 0.0, 1.0)
            for k in range(GROUP):
                dee[s0 + k, hs, :] = accs[k]
                u = accs[k] * wts[s0 + k, hs, :]
                u = u * u
                total = total + (u * fresh if k < again else u)
            return total

        return lax.fori_loop(0, steps, body, total)

    def share(k, total):
        rows[k, pl.ds(me, 1), :] = jnp.sum(total, axis=0, keepdims=True)
        for off in peers:
            pltpu.make_async_remote_copy(
                src_ref=rows.at[k, pl.ds(me, 1), :], dst_ref=rows.at[k, pl.ds(me, 1), :],
                send_sem=norm_send.at[k], recv_sem=norm_recv.at[k],
                device_id=at(off), device_id_type=MESH).start()

    def damped(k):
        all_rows(k).wait_recv()
        total = jnp.sum(jnp.sum(rows[k], axis=0, keepdims=True), axis=1, keepdims=True)
        return 1.0 / jnp.maximum(jnp.sqrt(total * (1.0 / entries)), 1.0)

    def all_rows(k):
        count = len(peers)
        return pltpu.make_async_remote_copy(
            src_ref=rows.at[k, pl.ds(0, count), :], dst_ref=rows.at[k, pl.ds(0, count), :],
            send_sem=norm_send.at[k], recv_sem=norm_recv.at[k],
            device_id=at(peers[0]), device_id_type=MESH)

    halves = [(0, pl.ds(0, 8)), (1, pl.ds(8, 8))]

    def newton(k, last, faces, with_mid=None, with_update=None):
        total = jnp.zeros((8, L), jnp.float32)
        for h, hs in halves:
            faces(h)
            chemistry(8 * h, 8)
            if k == 0 and h == 0:
                for cp in inv_loads:
                    cp.wait()
            total = matvec(h, total)
        if k == 0:
            pl.semaphore_wait(ready.at[1], len(lines[0]))
        share(k, total)
        r = damped(k)

        def mid(s):
            for h, hs in halves:
                z = base[s, hs, :] - dee[s, hs, :] * r
                zed[s, hs, :] = z
                put_tanh(s, h, z)

        species_loop(mid)
        if with_mid is not None:
            with_mid()
        chemistry()

        def second(s):
            for h, hs in halves:
                cbuf[cell_rows(s, h), :] += zed[s, hs, :] - base[s, hs, :]

        species_loop(second)
        share(k + 1, matvec(1, matvec(0, jnp.zeros((8, L), jnp.float32))))
        if with_update is not None:
            with_update()
        r2 = damped(k + 1)

        def end(s):
            for h, hs in halves:
                last(s, h, zed[s, hs, :] - dee[s, hs, :] * r2)

        species_loop(end)
        return r2

    tbuf[pl.ds(S * R, (SP - S) * R), :] = jnp.zeros(((SP - S) * R, L), jnp.float32)
    rpad[...] = jnp.zeros((SP, L), jnp.float32)
    rpad[0:S, 0:S] = -GAMMA * rates_ref[...]
    load.wait()
    pack(st, 0)
    pl.semaphore_wait(barrier, len(near))
    first_halo = halo_copies(st, 0, 0)
    for cp in first_halo[:1] + first_halo[2:]:
        cp.start()
    tell(0, lines[1])
    inner(st, e0)
    pl.semaphore_wait(ready.at[0], len(lines[1]))
    tell(1, lines[0])

    def weigh(s):
        wts[s] = 1.0 / (REL_TOL * jnp.abs(st[s]) + ABS_TOL)

    species_loop(weigh)
    first_halo[0].wait_send()
    first_halo[1].start()

    def fin0(s, h, e):
        hs = pl.ds(8 * h, 8)
        e0[s, hs, :] = e
        b = st[s, hs, :] + GAMMA * e
        base[s, hs, :] = b
        put_tanh(s, h, b)

    def faces0(h):
        if h == 0:
            for cp in first_halo[:1] + first_halo[2:]:
                cp.wait_recv()
            outer_z(0)
        else:
            first_halo[1].wait_recv()
        outer(0, h, e0, fin0)

    def keep(s, h, v):
        sec[s, pl.ds(8 * h, 8), :] = v
        put_tanh(s, h, v)

    early = (x_pair(zed, 0, EARLY, xlo.at[1], xhi.at[1], early_send, early_recv, 0)
             + x_pair(dee, 0, EARLY, dlo, dhi, early_send, early_recv, 2))

    def with_mid():
        for cp in early[:2]:
            cp.start()

    def with_update():
        for cp in early[2:]:
            cp.start()

    r2 = newton(0, keep, faces0, with_mid, with_update)

    second_halo = halo_copies(sec, 1, EARLY)
    second_halo[0].start()
    pack(sec, 1)
    for cp in second_halo[2:]:
        cp.start()
    inner(sec, ebuf)
    chemistry()

    def pre(s):
        for h, hs in halves:
            base[s, hs, :] = st[s, hs, :] + DELTA * e0[s, hs, :] + (1.0 - 1.0 / GAMMA) * cbuf[cell_rows(s, h), :]

    species_loop(pre)
    for cp in early:
        cp.wait()
    second_halo[0].wait_send()
    second_halo[1].start()

    def fin1(s, h, e):
        hs = pl.ds(8 * h, 8)
        b = base[s, hs, :] + (1.0 - DELTA) * e
        base[s, hs, :] = b
        put_tanh(s, h, b)

    def faces1(h):
        if h == 0:
            for cp in second_halo[:1] + second_halo[2:]:
                cp.wait_recv()
            outer_z(1)
        else:
            second_halo[1].wait_recv()
        outer(1, h, ebuf, fin1, r2)

    def give(s, h, v):
        out_ref[s, pl.ds(8 * h, 8), :] = v

    newton(2, give, faces1)
    for cp in first_halo[1:] + second_halo[1:]:
        cp.wait_send()
    for k in range(4):
        all_rows(k).wait_send()


def body(sizes, state, diffusivity, rates, inverse, boundary):
    shape = state.shape
    field = pltpu.VMEM((S, R, L), jnp.float32)
    faces = pltpu.VMEM((2, S, 8, L), jnp.float32)
    early = pltpu.VMEM((EARLY, 8, L), jnp.float32)
    n_all = sizes[0] * sizes[1] * sizes[2]
    out = pl.pallas_call(
        functools.partial(kernel, sizes),
        name="ark_step",
        out_shape=jax.ShapeDtypeStruct((S, R, L), jnp.float32),
        in_specs=[
            pl.BlockSpec(memory_space=pltpu.HBM) for _ in range(5)
        ],
        out_specs=pl.BlockSpec(memory_space=pltpu.VMEM),
        scratch_shapes=[
            pltpu.SMEM((S,), jnp.float32), pltpu.VMEM((S, S), jnp.float32), pltpu.SMEM((3,), jnp.int32),
            field, pltpu.VMEM((S, S, R, L), jnp.float32),
            faces, faces, early, early, faces, faces, faces, faces,
            pltpu.VMEM((2, 32, L), jnp.float32), pltpu.VMEM((32, L), jnp.float32),
            pltpu.VMEM((2, 32, L), jnp.float32), pltpu.VMEM((2, 32, L), jnp.float32),
            field, field, field, field, field, field, field,
            pltpu.VMEM((SP * R, L), jnp.float32), pltpu.VMEM((SP * R, L), jnp.float32),
            pltpu.VMEM((SP, L), jnp.float32), pltpu.VMEM((4, n_all, L), jnp.float32),
            pltpu.SemaphoreType.DMA((4,)), pltpu.SemaphoreType.DMA((CHUNKS,)),
            pltpu.SemaphoreType.DMA((2, 6)), pltpu.SemaphoreType.DMA((2, 6)),
            pltpu.SemaphoreType.DMA((4,)), pltpu.SemaphoreType.DMA((4,)),
            pltpu.SemaphoreType.DMA((4,)), pltpu.SemaphoreType.DMA((4,)), pltpu.SemaphoreType.REGULAR((2,)),
        ],
        compiler_params=pltpu.CompilerParams(collective_id=0, has_side_effects=True, vmem_limit_bytes=48 << 20),
    )(
        *[pltpu.with_memory_space_constraint(a, pltpu.HBM) for a in (
            state.reshape(S, R, L), diffusivity, rates, inverse.reshape(S, S, R, L), boundary)],
    )
    return out.reshape(shape)


def solution(mesh):
    sizes = tuple(mesh.shape[a] for a in AXES)
    in_specs = (P(None, "gx", "gy", "gz"), P(), P(), P(None, None, "gx", "gy", "gz"), P())
    return jax.shard_map(
        functools.partial(body, sizes), mesh=mesh, in_specs=in_specs, out_specs=P(None, "gx", "gy", "gz"), check_vma=False)
```

```python
import functools
import itertools

import jax
import jax.numpy as jnp
from jax import lax
from jax.experimental import pallas as pl
from jax.experimental.pallas import tpu as pltpu
from jax.sharding import PartitionSpec as P

MESH = pl.DeviceIdType.MESH
AXES = ("gx", "gy", "gz")

GAMMA = 0.2928932188134524
DELTA = -0.7071067811865475
REL_TOL = 0.1
ABS_TOL = 0.05
DRIFT = 0.2

S = 53
SP = 64
R = 16
L = 128
GROUP = 18
JB = 13
EARLY = 17
CHUNKS = 8


def offsets(sizes):
    out = []
    for off in itertools.product(*[range(n) for n in sizes]):
        if any(off):
            out.append(off)

    def hops(off):
        gx, gy, gz = off
        ring = lambda d, n: min(d % n, n - d % n)
        far_y = ring(gy, sizes[1])
        far_z = ring(gx // 2, sizes[0] // 2)
        far_x = ring(2 * (gx % 2) + gz // 2, 4)
        return far_x + far_y + far_z

    return sorted(out, key=lambda off: -hops(off))


def species_loop(fn, block=8):
    whole = S // block

    def body(i, carry):
        for k in range(block):
            fn(i * block + k)
        return carry

    lax.fori_loop(0, whole, body, 0)
    for s in range(whole * block, S):
        fn(s)


def block_loop(fn, block=16, unroll=False):
    whole = S // block
    if unroll:
        for i in range(whole + 1):
            fn(i, list(range(i * block, min(S, (i + 1) * block))))
        return

    def body(i, carry):
        fn(i, [i * block + k for k in range(block)])
        return carry

    lax.fori_loop(0, whole, body, 0)
    fn(whole, list(range(whole * block, S)))


def tile8(i):
    return pl.ds(8 * i if isinstance(i, int) else pl.multiple_of(8 * i, 8), 8)


def kernel(
    sizes,
    state_hbm, diff_hbm, rates_hbm, inv_hbm, bound_hbm,
    out_ref,
    diff_ref, rates_ref, bound_ref, st, inv, xlo, xhi, dlo, dhi, ya, yb, yra, yrb, zp, zk, zlo, zhi,
    e0, ebuf, wts, base, zed, sec, dee, tbuf, cbuf, rpad, rows,
    load_sem, inv_sem, halo_send, halo_recv, early_send, early_recv, norm_send, norm_recv, ready,
):
    n_all = sizes[0] * sizes[1] * sizes[2]
    entries = float(S * R * L * n_all)
    pos = [lax.axis_index(a) for a in AXES]
    me = (pos[0] * sizes[1] + pos[1]) * sizes[2] + pos[2]

    def at(off):
        return {a: lax.rem(p + o, n) for a, p, o, n in zip(AXES, pos, off, sizes)}

    peers = offsets(sizes)

    ahead = [(1, 0, 0), (0, 1, 0), (0, 0, 1)]
    back = [tuple((sizes[d] - 1) * o for d, o in enumerate(off)) for off in ahead]

    barrier = pltpu.get_barrier_semaphore()
    lines = [[tuple(o if a == d else 0 for a in range(3)) for o in range(1, sizes[d])] for d in range(3)]
    near = lines[0] + lines[1] + lines[2]
    for off in ahead[:1] + back[:1] + [o for o in near if o not in (ahead[0], back[0])]:
        pl.semaphore_signal(barrier, inc=1, device_id=at(off), device_id_type=MESH)

    load = pltpu.make_async_copy(state_hbm, st, load_sem.at[0])
    load.start()
    small = [pltpu.make_async_copy(src, dst, load_sem.at[i]) for i, (src, dst) in enumerate(
        [(diff_hbm, diff_ref), (rates_hbm, rates_ref), (bound_hbm, bound_ref)], 1)]
    for cp in small:
        cp.start()
    per = -(-S // CHUNKS)
    inv_loads = []
    for c in range(CHUNKS):
        lo, hi = c * per, min(S, (c + 1) * per)
        cp = pltpu.make_async_copy(inv_hbm.at[pl.ds(lo, hi - lo)], inv.at[pl.ds(lo, hi - lo)], inv_sem.at[c])
        cp.start()
        inv_loads.append(cp)

    def tell(i, line):
        for off in line:
            pl.semaphore_signal(ready.at[i], inc=1, device_id=at(off), device_id_type=MESH)

    for cp in small:
        cp.wait()

    row = lax.broadcasted_iota(jnp.int32, (8, L), 0)
    lane = lax.broadcasted_iota(jnp.int32, (8, L), 1)
    yy = lax.rem(row, 4)
    pp = lax.rem(lane, 4)
    f = lambda c: jnp.where(c, 1.0, 0.0).astype(jnp.float32)
    low_rows = f(row < 4)
    high_rows = f(row >= 4)

    def wall(d, edge):
        return jnp.where((bound_ref[d] == 0) & (pos[d] == edge), 1.0, 0.0).astype(jnp.float32)

    wx0, wx1 = wall(0, 0), wall(0, sizes[0] - 1)
    wy0, wy1 = wall(1, 0), wall(1, sizes[1] - 1)
    wz0, wz1 = wall(2, 0), wall(2, sizes[2] - 1)
    mx0, mx1, my0, my1, mz0, mz1 = [1.0 - w for w in (wx0, wx1, wy0, wy1, wz0, wz1)]

    rd = lambda ref, s, h: ref[s, pl.ds(8 * h, 8), :]

    grp = lane // 4

    def pack(field, k):
        def some(i, species):
            acc = jnp.zeros((8, L), jnp.float32)
            for g, s in enumerate(species):
                v0, v1 = rd(field, s, 0), rd(field, s, 1)
                ya[k, s] = jnp.where(yy < 2, pltpu.roll(v0, 6, 0), v1)
                yb[k, s] = jnp.where(yy < 2, v0, pltpu.roll(v1, 2, 0))
                acc = jnp.where(grp == 2 * g, pltpu.roll(v0, (8 * g + 2) % L, 1), acc)
                acc = jnp.where(grp == 2 * g + 1, pltpu.roll(v1, (8 * g + 6) % L, 1), acc)
            zp[k, tile8(i), :] = acc

        block_loop(some)

    def remote(src, dst, off, send, recv):
        return pltpu.make_async_remote_copy(
            src_ref=src, dst_ref=dst, send_sem=send, recv_sem=recv, device_id=at(off), device_id_type=MESH)

    def x_pair(field, first, count, lo, hi, sends, recvs, i):
        some = pl.ds(first, count)
        return [
            remote(field.at[some, pl.ds(8, 8), :], lo.at[some], ahead[0], sends.at[i], recvs.at[i]),
            remote(field.at[some, pl.ds(0, 8), :], hi.at[some], back[0], sends.at[i + 1], recvs.at[i + 1]),
        ]

    def halo_copies(field, k, first):
        todo = [
            (zp.at[k], zlo.at[k], ahead[2]),
            (zp.at[k], zhi.at[k], back[2]),
            (ya.at[k], yra.at[k], ahead[1]),
            (yb.at[k], yrb.at[k], back[1]),
        ]
        cps = x_pair(field, first, S - first, xlo.at[k], xhi.at[k], halo_send.at[k], halo_recv.at[k], 0)
        for i, (src, dst, off) in enumerate(todo, 2):
            cps.append(remote(src, dst, off, halo_send.at[k, i], halo_recv.at[k, i]))
        return cps

    def inner(field, out):
        x0c = -30.0 + 16.0 * wx0 * low_rows
        x1c = -30.0 + 16.0 * wx1 * high_rows
        b1 = 16.0 * f(yy >= 1) - wy0 * f(yy == 1) - wy1 * f(yy == 3)
        bm1 = 16.0 * f(yy <= 2) - wy0 * f(yy == 0) - wy1 * f(yy == 2)
        b2, bm2 = -f(yy >= 2), -f(yy <= 1)
        a1 = 16.0 * f(lane >= 1) - wz0 * f(lane == 1) - wz1 * f(lane == L - 1)
        am1 = 16.0 * f(lane <= L - 2) - wz0 * f(lane == 0) - wz1 * f(lane == L - 2)
        a2, am2 = -f(lane >= 2), -f(lane <= L - 3)
        yz0 = (-60.0 + 16.0 * wy0 * f(yy == 0) + 16.0 * wy1 * f(yy == 3)
               + 16.0 * wz0 * f(lane == 0) + 16.0 * wz1 * f(lane == L - 1))
        own_drift = -DRIFT + DRIFT * wx0 * low_rows

        def one(s):
            c = diff_ref[s] * (1.0 / 12.0)
            v0, v1 = rd(field, s, 0), rd(field, s, 1)
            s0, s1 = pltpu.roll(v0, 4, 0), pltpu.roll(v1, 4, 0)

            def yz(v):
                return (yz0 * v + b1 * pltpu.roll(v, 1, 0) + b2 * pltpu.roll(v, 2, 0)
                        + bm1 * pltpu.roll(v, 7, 0) + bm2 * pltpu.roll(v, 6, 0)
                        + a1 * pltpu.roll(v, 1, 1) + a2 * pltpu.roll(v, 2, 1)
                        + am1 * pltpu.roll(v, L - 1, 1) + am2 * pltpu.roll(v, L - 2, 1))

            l0 = x0c * v0 + (16.0 - wx0) * s0 + 16.0 * high_rows * s1 - v1 + yz(v0)
            l1 = x1c * v1 + (16.0 - wx1) * s1 + 16.0 * low_rows * s0 - v0 + yz(v1)
            out[s, pl.ds(0, 8), :] = c * l0 + own_drift * v0 + DRIFT * high_rows * s0
            out[s, pl.ds(8, 8), :] = c * l1 - DRIFT * v1 + DRIFT * jnp.where(row >= 4, s1, s0)

        species_loop(one, 4)

    def outer_z(k):
        for q in range(4):
            lo = zlo[k, pl.ds(8 * q, 8), :]
            hi = zhi[k, pl.ds(8 * q, 8), :]
            from_hi = mz1 * (16.0 * f(pp == 1) * pltpu.roll(hi, L - 1, 1) - pltpu.roll(hi, L - 2, 1))
            from_lo = mz0 * (16.0 * f(pp == 2) * pltpu.roll(lo, 1, 1) - pltpu.roll(lo, 2, 1))
            zk[pl.ds(8 * q, 8), :] = jnp.where(pp < 2, from_hi, from_lo)

    def outer(k, h, part, fin, r=None):
        edge = (lane < 2) | (lane >= L - 2)
        even = 16.0 * my0 * f(lax.rem(row, 2) == 0)
        odd = 16.0 * my1 * f(lax.rem(row, 2) == 1)
        lo16, hi16, dr = 16.0 * mx0 * low_rows, 16.0 * mx1 * high_rows, DRIFT * mx0 * low_rows

        def some(i, species):
            zt = zk[tile8(i), :]
            for g, s in enumerate(species):
                c = diff_ref[s] * (1.0 / 12.0)
                a, b = yra[k, s], yrb[k, s]
                ca = even * pltpu.roll(a, 7, 0) - my0 * a
                cb = odd * pltpu.roll(b, 1, 0) - my1 * b
                z = jnp.where(edge, pltpu.roll(zt, (2 * L - 2 - 8 * g - 4 * h) % L, 1), 0.0)
                if h == 0:
                    x = xlo[k, s]
                    if r is not None and s < EARLY:
                        x = x - dlo[s] * r
                    turned = pltpu.roll(x, 4, 0)
                    lap = lo16 * turned - mx0 * x + jnp.where(yy < 2, ca, pltpu.roll(cb, 2, 0)) + z
                    fin(s, h, rd(part, s, h) + c * lap + dr * turned)
                else:
                    x = xhi[k, s]
                    if r is not None and s < EARLY:
                        x = x - dhi[s] * r
                    lap = hi16 * pltpu.roll(x, 4, 0) - mx1 * x + jnp.where(yy < 2, pltpu.roll(ca, 6, 0), cb) + z
                    fin(s, h, rd(part, s, h) + c * lap)

        block_loop(some, unroll=r is not None)

    def cell_rows(s, h):
        start = s * R + 8 * h
        return pl.ds(start if isinstance(start, int) else pl.multiple_of(start, 8), 8)

    def put_tanh(s, h, v):
        tbuf[cell_rows(s, h), :] = jnp.tanh(v)

    def chemistry(first=0, rows_done=R):
        lhs = rows_lhs()
        for r in range(first, first + rows_done, 2):
            t = jnp.concatenate([tbuf[pl.ds(r + i, SP, stride=R), :] for i in range(2)], axis=1)
            hi = t.astype(jnp.bfloat16)
            lo = (t - hi.astype(jnp.float32)).astype(jnp.bfloat16)
            got = jnp.dot(lhs, jnp.concatenate([hi, lo, hi, lo], axis=0), preferred_element_type=jnp.float32)
            for i in range(2):
                cbuf[pl.ds(r + i, SP, stride=R), :] = got[:, i * L:(i + 1) * L]

    def rows_lhs():
        both = rpad[...] + pltpu.roll(rpad[...], SP, 1)
        hi = both.astype(jnp.bfloat16)
        lo = (both - hi.astype(jnp.float32)).astype(jnp.bfloat16)
        return jnp.concatenate([hi, lo], axis=1)

    def matvec(h, total):
        last = S - GROUP
        steps = -(-S // GROUP)
        again = steps * GROUP - S
        hs = pl.ds(8 * h, 8)

        def columns(s0, j0, count, accs):
            accs = list(accs)
            for jj in range(count):
                g = cbuf[cell_rows(j0 + jj, h), :]
                for k in range(GROUP):
                    accs[k] = accs[k] + inv[s0 + k, j0 + jj, hs, :] * g
            return tuple(accs)

        def body(i, total):
            s0 = jnp.minimum(i * GROUP, last)
            accs = tuple(jnp.zeros((8, L), jnp.float32) for _ in range(GROUP))
            accs = lax.fori_loop(0, S // JB, lambda t, acc: columns(s0, t * JB, JB, acc), accs)
            accs = columns(s0, S // JB * JB, S % JB, accs)
            fresh = jnp.where(i == steps - 1, 0.0, 1.0)
            for k in range(GROUP):
                dee[s0 + k, hs, :] = accs[k]
                u = accs[k] * wts[s0 + k, hs, :]
                u = u * u
                total = total + (u * fresh if k < again else u)
            return total

        return lax.fori_loop(0, steps, body, total)

    def share(k, total):
        rows[k, pl.ds(me, 1), :] = jnp.sum(total, axis=0, keepdims=True)
        for off in peers:
            pltpu.make_async_remote_copy(
                src_ref=rows.at[k, pl.ds(me, 1), :], dst_ref=rows.at[k, pl.ds(me, 1), :],
                send_sem=norm_send.at[k], recv_sem=norm_recv.at[k],
                device_id=at(off), device_id_type=MESH).start()

    def damped(k):
        all_rows(k).wait_recv()
        total = jnp.sum(jnp.sum(rows[k], axis=0, keepdims=True), axis=1, keepdims=True)
        return 1.0 / jnp.maximum(jnp.sqrt(total * (1.0 / entries)), 1.0)

    def all_rows(k):
        count = len(peers)
        return pltpu.make_async_remote_copy(
            src_ref=rows.at[k, pl.ds(0, count), :], dst_ref=rows.at[k, pl.ds(0, count), :],
            send_sem=norm_send.at[k], recv_sem=norm_recv.at[k],
            device_id=at(peers[0]), device_id_type=MESH)

    halves = [(0, pl.ds(0, 8)), (1, pl.ds(8, 8))]

    def newton(k, last, faces, with_mid=None, with_update=None):
        total = jnp.zeros((8, L), jnp.float32)
        for h, hs in halves:
            faces(h)
            chemistry(8 * h, 8)
            if k == 0 and h == 0:
                for cp in inv_loads:
                    cp.wait()
            total = matvec(h, total)
        if k == 0:
            pl.semaphore_wait(ready.at[1], len(lines[0]))
        share(k, total)
        r = damped(k)

        def mid(s):
            for h, hs in halves:
                z = base[s, hs, :] - dee[s, hs, :] * r
                zed[s, hs, :] = z
                put_tanh(s, h, z)

        species_loop(mid)
        if with_mid is not None:
            with_mid()
        chemistry()

        def second(s):
            for h, hs in halves:
                cbuf[cell_rows(s, h), :] += zed[s, hs, :] - base[s, hs, :]

        species_loop(second)
        share(k + 1, matvec(1, matvec(0, jnp.zeros((8, L), jnp.float32))))
        if with_update is not None:
            with_update()
        r2 = damped(k + 1)

        def end(s):
            for h, hs in halves:
                last(s, h, zed[s, hs, :] - dee[s, hs, :] * r2)

        species_loop(end)
        return r2

    tbuf[pl.ds(S * R, (SP - S) * R), :] = jnp.zeros(((SP - S) * R, L), jnp.float32)
    rpad[...] = jnp.zeros((SP, L), jnp.float32)
    rpad[0:S, 0:S] = -GAMMA * rates_ref[...]
    load.wait()
    pack(st, 0)
    pl.semaphore_wait(barrier, len(near))
    first_halo = halo_copies(st, 0, 0)
    for cp in first_halo[:1] + first_halo[2:]:
        cp.start()
    tell(0, lines[1])
    inner(st, e0)

    def weigh(s):
        wts[s] = 1.0 / (REL_TOL * jnp.abs(st[s]) + ABS_TOL)

    species_loop(weigh)
    first_halo[0].wait_send()
    first_halo[1].start()
    pl.semaphore_wait(ready.at[0], len(lines[1]))
    tell(1, lines[0])

    def fin0(s, h, e):
        hs = pl.ds(8 * h, 8)
        e0[s, hs, :] = e
        b = st[s, hs, :] + GAMMA * e
        base[s, hs, :] = b
        put_tanh(s, h, b)

    def faces0(h):
        if h == 0:
            for cp in first_halo[:1] + first_halo[2:]:
                cp.wait_recv()
            outer_z(0)
        else:
            first_halo[1].wait_recv()
        outer(0, h, e0, fin0)

    def keep(s, h, v):
        sec[s, pl.ds(8 * h, 8), :] = v

    early = (x_pair(zed, 0, EARLY, xlo.at[1], xhi.at[1], early_send, early_recv, 0)
             + x_pair(dee, 0, EARLY, dlo, dhi, early_send, early_recv, 2))

    def with_mid():
        for cp in early[:2]:
            cp.start()

    def with_update():
        for cp in early[2:]:
            cp.start()

    r2 = newton(0, keep, faces0, with_mid, with_update)

    second_halo = halo_copies(sec, 1, EARLY)
    second_halo[0].start()
    pack(sec, 1)
    for cp in second_halo[2:]:
        cp.start()

    def section_tanh(s):
        for h, hs in halves:
            put_tanh(s, h, sec[s, hs, :])

    species_loop(section_tanh)
    inner(sec, ebuf)
    chemistry()

    def pre(s):
        for h, hs in halves:
            base[s, hs, :] = st[s, hs, :] + DELTA * e0[s, hs, :] + (1.0 - 1.0 / GAMMA) * cbuf[cell_rows(s, h), :]

    species_loop(pre)
    for cp in early:
        cp.wait()
    second_halo[0].wait_send()
    second_halo[1].start()

    def fin1(s, h, e):
        hs = pl.ds(8 * h, 8)
        b = base[s, hs, :] + (1.0 - DELTA) * e
        base[s, hs, :] = b
        put_tanh(s, h, b)

    def faces1(h):
        if h == 0:
            for cp in second_halo[:1] + second_halo[2:]:
                cp.wait_recv()
            outer_z(1)
        else:
            second_halo[1].wait_recv()
        outer(1, h, ebuf, fin1, r2)

    def give(s, h, v):
        out_ref[s, pl.ds(8 * h, 8), :] = v

    newton(2, give, faces1)
    for cp in first_halo[1:] + second_halo[1:]:
        cp.wait_send()
    for k in range(4):
        all_rows(k).wait_send()


def body(sizes, state, diffusivity, rates, inverse, boundary):
    shape = state.shape
    field = pltpu.VMEM((S, R, L), jnp.float32)
    faces = pltpu.VMEM((2, S, 8, L), jnp.float32)
    early = pltpu.VMEM((EARLY, 8, L), jnp.float32)
    n_all = sizes[0] * sizes[1] * sizes[2]
    out = pl.pallas_call(
        functools.partial(kernel, sizes),
        name="ark_step",
        out_shape=jax.ShapeDtypeStruct((S, R, L), jnp.float32),
        in_specs=[
            pl.BlockSpec(memory_space=pltpu.HBM) for _ in range(5)
        ],
        out_specs=pl.BlockSpec(memory_space=pltpu.VMEM),
        scratch_shapes=[
            pltpu.SMEM((S,), jnp.float32), pltpu.VMEM((S, S), jnp.float32), pltpu.SMEM((3,), jnp.int32),
            field, pltpu.VMEM((S, S, R, L), jnp.float32),
            faces, faces, early, early, faces, faces, faces, faces,
            pltpu.VMEM((2, 32, L), jnp.float32), pltpu.VMEM((32, L), jnp.float32),
            pltpu.VMEM((2, 32, L), jnp.float32), pltpu.VMEM((2, 32, L), jnp.float32),
            field, field, field, field, field, field, field,
            pltpu.VMEM((SP * R, L), jnp.float32), pltpu.VMEM((SP * R, L), jnp.float32),
            pltpu.VMEM((SP, L), jnp.float32), pltpu.VMEM((4, n_all, L), jnp.float32),
            pltpu.SemaphoreType.DMA((4,)), pltpu.SemaphoreType.DMA((CHUNKS,)),
            pltpu.SemaphoreType.DMA((2, 6)), pltpu.SemaphoreType.DMA((2, 6)),
            pltpu.SemaphoreType.DMA((4,)), pltpu.SemaphoreType.DMA((4,)),
            pltpu.SemaphoreType.DMA((4,)), pltpu.SemaphoreType.DMA((4,)), pltpu.SemaphoreType.REGULAR((2,)),
        ],
        compiler_params=pltpu.CompilerParams(collective_id=0, has_side_effects=True, vmem_limit_bytes=48 << 20),
    )(
        *[pltpu.with_memory_space_constraint(a, pltpu.HBM) for a in (
            state.reshape(S, R, L), diffusivity, rates, inverse.reshape(S, S, R, L), boundary)],
    )
    return out.reshape(shape)


def solution(mesh):
    sizes = tuple(mesh.shape[a] for a in AXES)
    in_specs = (P(None, "gx", "gy", "gz"), P(), P(), P(None, None, "gx", "gy", "gz"), P())
    return jax.shard_map(
        functools.partial(body, sizes), mesh=mesh, in_specs=in_specs, out_specs=P(None, "gx", "gy", "gz"), check_vma=False)
```
